128 devices in a mesh: sec: 2 (over y_hi), rr: 8 (over y_lo, z), sr: 8 (over x, core).
Axes of the slice: x: 4, y: 4 (y_hi: 2, y_lo: 2; y = y_hi * 2 + y_lo), z: 4, core: 2. Of those that a mesh axis runs over, the one named last changes fastest.
Arguments:
- wave_prev: float32 [2, 4, 256, 256, 256], P('sec', None, 'rr', 'sr'), may hold values from -6 to 6
- wave_now: float32 [2, 4, 256, 256, 256], P('sec', None, 'rr', 'sr'), may hold values from -6 to 6
- potential: float32 [2, 256, 256, 256], P('sec', 'rr', 'sr'), may hold values from -0.5 to 0.5
- damping: float32 [2, 256, 256], P('sec', 'rr', 'sr'), may hold values from 0.7 to 1
- switch: float32 [256, 256], P('rr', 'sr'), may hold values from 0.05 to 0.5
- angular: float32 [2, 4, 256, 256], P('sec')
- coriolis: float32 [2, 3, 256, 256], P('sec'), may hold values from -0.375 to 0.375
- helicity_start: int32 [2], P('sec'), may hold values from 0 to 20
- frame_map: float32 [4, 256, 4, 256], replicated, may hold values from -0.1875 to 0.1875
- route_table: int32 [64, 64, 2], replicated, may hold values from -1 to 127, as said below
- pick_slots: int32 [8, 8, 128, 4], P('rr', 'sr'), may hold values from 0 to 127, as said below
- interp_weights: float32 [8, 8, 128, 4, 8, 8], P('rr', 'sr'), may hold values from -1 to 1
Outputs:
- wave_prev_out: float32 [2, 4, 256, 256, 256], P('sec', None, 'rr', 'sr')
- wave_now_out: float32 [2, 4, 256, 256, 256], P('sec', None, 'rr', 'sr')
The draws below stay inside these ranges and needn't reach their ends.
Inputs may be any that keep to these rules, and one draw needn't show every extreme that they name: route_table[d, s, t] is the block of reactant slab s sent to product slab d in slot t, or -1; the filled slots of a pair come first and name different blocks; every product slab gets 2 blocks from some slab, and some product slab gets 2 blocks from every slab. Each entry e2 of pick_slots[d] has route_table[d, e2 // 2, e2 % 2] >= 0, and every such filled slot of d is named by some entry.
All inputs are finite; a program needn't handle non-finite values.
Results may differ from the reference program's by a relative error of at most 0.0003.
Values sent between devices are 32-bit elements; how exact they have to be, the bound alone decides.
No kernel may reach another device: no remote copies, remote signals or barrier semaphores. Data moves between devices by JAX's collectives and lax.ppermute only.
A program may use at most 128 MiB of HBM per device.

```python
import jax
import jax.numpy as jnp
from jax import lax

HEL = 4
NA = 256
JTOT = 23
CR = 32
CS = 32
STEPS = 2
BLOCK = 8
MSLOT = 4
CAP = 2
SLAB_R = 8
SLAB_S = 8
SRCS = 64
NR = 256
NS = 256
NBLK = 128


def plan_tables(key):
    sources = SLAB_R * SLAB_S
    base_key = jax.random.fold_in(key, 4242)
    subkeys = jax.random.split(base_key, 6)
    counts = jax.random.randint(subkeys[0], (sources, sources), 0, CAP + 1)
    dest_index = jnp.arange(sources)[:, None]
    source_index = jnp.arange(sources)[None, :]
    full_dest = jax.random.randint(subkeys[1], (), 0, sources)
    offset = jax.random.randint(subkeys[2], (), 0, sources)
    counts = jnp.where(dest_index == full_dest, CAP, counts)
    counts = jnp.where(source_index == (dest_index + offset) % sources, CAP, counts)
    first_block = jax.random.randint(subkeys[3], (sources, sources, 1), 0, NBLK)
    stride = jax.random.randint(subkeys[4], (sources, sources, 1), 1, NBLK // CAP + 1)
    slot_index = jnp.arange(CAP)[None, None, :]
    block_ids = (first_block + slot_index * stride) % NBLK
    filled = slot_index < counts[:, :, None]
    route_table = jnp.where(filled, block_ids, -1).astype(jnp.int32)
    filled_flat = filled.reshape(sources, sources * CAP).astype(jnp.int32)
    shuffles = jax.vmap(lambda piece_key: jax.random.permutation(piece_key, sources * CAP))(jax.random.split(subkeys[5], sources))
    ranking = (1 - filled_flat) * (sources * CAP) + shuffles
    ordering = jnp.argsort(ranking, axis=1)
    totals = jnp.sum(filled_flat, axis=1)
    cyclic_walk = jnp.arange(NBLK)[:, None] + jnp.arange(MSLOT)[None, :] * NBLK
    position = cyclic_walk[None, :, :] % totals[:, None, None]
    pick_slots = jnp.take_along_axis(ordering, position.reshape(sources, NBLK * MSLOT), axis=1)
    return (route_table, pick_slots.reshape(SLAB_R, SLAB_S, NBLK, MSLOT).astype(jnp.int32))


def draw_route_table(key, part):
    return plan_tables(key)[0]


def draw_pick_slots(key, part):
    return plan_tables(key)[1]


def draw_angular(key, part):
    array_shape = (2, HEL, NA, NA)
    samples = jax.random.normal(key, array_shape, jnp.float32)
    symmetric = (samples + jnp.swapaxes(samples, -1, -2)) * 0.5 ** 0.5 * NA ** (-0.5)
    return symmetric.astype(jnp.float32)


def level_of(rng, extent, cuts, smallest, top_value):
    factor_of, own = 1.0, jax.random.fold_in(rng, 6)
    for dim, parts in cuts:
        draws = jnp.exp(jax.random.uniform(jax.random.fold_in(own, dim), (parts,), jnp.float32, smallest / len(cuts), top_value / len(cuts)))
        factor_of = factor_of * jnp.repeat(draws, extent[dim] // parts).reshape([-1 if axis == dim else 1 for axis in range(len(extent))])
    return factor_of


def gaussian(rng, dims, width, most, pieces=(), kind=jnp.bfloat16):
    array = jax.random.normal(rng, dims, jnp.float32) * width
    if len(pieces) > 0:
        array = level_of(rng, dims, pieces, -0.22, 0.18) * array
    return jnp.clip(array, min=-most, max=most).astype(kind)


def setup_inputs(seed: int = 0) -> dict:
    streams_of = jax.random.split(jax.random.key(seed), 13)
    wave_prev = gaussian(streams_of[0], (2, HEL, NR, NS, NA), 1.0, 6.0, ((0, 2), (2, 8), (3, 8)), jnp.float32)
    wave_now = gaussian(streams_of[1], (2, HEL, NR, NS, NA), 1.0, 6.0, ((0, 2), (2, 8), (3, 8)), jnp.float32)
    potential = jnp.clip(jax.random.uniform(streams_of[2], (2, NR, NS, NA), jnp.float32, -0.5, 0.5) * level_of(streams_of[2], (2, NR, NS, NA), ((0, 2), (1, 8), (2, 8)), -0.4, 0.0), -0.5, 0.5)
    damping = jnp.clip(0.7 + 0.3 * jax.random.uniform(streams_of[3], (2, NR, NS), jnp.float32) ** level_of(streams_of[3], (2, NR, NS), ((0, 2), (1, 8), (2, 8)), -0.2, 0.2), 0.7, 1.0)
    switch = jnp.clip(0.05 + 0.45 * jax.random.uniform(streams_of[4], (NR, NS), jnp.float32) ** level_of(streams_of[4], (NR, NS), ((0, 8), (1, 8)), -0.2, 0.2), 0.05, 0.5)
    angular = draw_angular(jax.random.fold_in(streams_of[12], 71), 0)
    coriolis = gaussian(streams_of[6], (2, HEL - 1, NA, NA), NA ** -0.5, 0.375, ((0, 2),), jnp.float32)
    helicity_start = jax.random.randint(streams_of[7], (2,), 0, JTOT - HEL + 2).astype(jnp.int32)
    frame_map = gaussian(streams_of[8], (HEL, NA, HEL, NA), (HEL * NA) ** -0.5, 0.1875, (), jnp.float32)
    route_table = draw_route_table(jax.random.fold_in(streams_of[12], 71), 0)
    pick_slots = draw_pick_slots(jax.random.fold_in(streams_of[12], 71), 0)
    interp_weights = gaussian(streams_of[11], (SLAB_R, SLAB_S, NBLK, MSLOT, BLOCK, BLOCK), (MSLOT * BLOCK) ** -0.5, 1.0, ((0, 8), (1, 8)), jnp.float32)
    return dict(wave_prev=wave_prev, wave_now=wave_now, potential=potential, damping=damping, switch=switch, angular=angular, coriolis=coriolis, helicity_start=helicity_start, frame_map=frame_map, route_table=route_table, pick_slots=pick_slots, interp_weights=interp_weights)


kinetic_radial = 0.08
kinetic_bond = 0.08
rotor_scale = 0.1
centrifugal = 0.0005
coriolis_scale = 0.005
highest = lax.Precision.HIGHEST

def hamilton(state_field, angles, coupling, potent, radial, bond_factor, helicity_vals):
    padded = jnp.pad(state_field, ((0, 0), (1, 1), (1, 1), (0, 0)))
    laplace = kinetic_radial * (2.0 * state_field - padded[:, 2:, 1:-1] - padded[:, :-2, 1:-1])
    laplace = laplace + kinetic_bond * (2.0 * state_field - padded[:, 1:-1, 2:] - padded[:, 1:-1, :-2])
    rotated = jnp.einsum('kijb,kab->kija', state_field, angles, precision=highest, preferred_element_type=jnp.float32)
    total_j = float(JTOT * (JTOT + 1))
    ladder = jnp.sqrt(total_j - helicity_vals * (helicity_vals + 1.0))[:-1]
    raised = jnp.einsum('kijb,kab->kija', state_field[1:], coupling, precision=highest, preferred_element_type=jnp.float32) * ladder[:, None, None, None]
    lowered = jnp.einsum('kijb,kba->kija', state_field[:-1], coupling, precision=highest, preferred_element_type=jnp.float32) * ladder[:, None, None, None]
    blank_row = jnp.zeros_like(state_field[:1])
    mixing = jnp.concatenate([raised, blank_row], 0) + jnp.concatenate([blank_row, lowered], 0)
    centre_term = centrifugal * (total_j - 2.0 * helicity_vals * helicity_vals)
    rotation = rotor_scale * (radial[:, None] + bond_factor[None, :])
    return laplace + rotation[None, :, :, None] * rotated + radial[None, :, None, None] * (centre_term[:, None, None, None] * state_field + coriolis_scale * mixing) + potent[None] * state_field

def transfer(absorbed, frame_map, route_table, pick_slots, interp_weights):
    blocks = absorbed.reshape(HEL, SLAB_R, CR, SLAB_S, CS, NA).transpose(0, 1, 3, 2, 4, 5).reshape(HEL, SRCS * NBLK, BLOCK, NA)
    picks = pick_slots.reshape(SRCS, NBLK, MSLOT)
    weights = interp_weights.reshape(SRCS, NBLK, MSLOT, BLOCK, BLOCK)

    def destination(inputs):
        table, chosen, blend = inputs
        source = chosen // CAP
        within = chosen % CAP
        local_id = table[source, within]
        filled = local_id >= 0
        global_id = (source * NBLK + jnp.maximum(local_id, 0)).astype(jnp.int32)
        selected = jnp.take(blocks, global_id, axis=1)
        selected = jnp.where(filled[None, :, :, None, None], selected, 0.0)
        blended = jnp.einsum('bmij,kbmja->kbia', blend, selected, precision=highest, preferred_element_type=jnp.float32)
        row_values = blended.reshape(HEL, CR * CS, NA)
        return jnp.einsum('kna,kalb->lnb', row_values, frame_map, precision=highest, preferred_element_type=jnp.float32)
    outcome = lax.map(destination, (route_table, picks, weights))
    return outcome.reshape(SLAB_R, SLAB_S, HEL, CR, CS, NA).transpose(2, 0, 3, 1, 4, 5).reshape(HEL, NR, NS, NA)

def reference(wave_prev, wave_now, potential, damping, switch, angular, coriolis, helicity_start, frame_map, route_table, pick_slots, interp_weights):
    radial = (1.0 + 3.0 * jnp.arange(NR, dtype=jnp.float32) / float(NR)) ** (-2)
    bond_factor = (1.0 + 3.0 * jnp.arange(NS, dtype=jnp.float32) / float(NS)) ** (-2)
    previous = wave_prev
    current = wave_now
    for iteration in range(STEPS):
        renewed = []
        for section in range(2):
            helicity_vals = helicity_start[section].astype(jnp.float32) + jnp.arange(HEL, dtype=jnp.float32)
            applied = hamilton(current[section], angular[section], coriolis[section], potential[section], radial, bond_factor, helicity_vals)
            damp_grid = damping[section][None, :, :, None]
            renewed.append(damp_grid * (2.0 * applied - damp_grid * previous[section]))
        absorbed = switch[None, :, :, None] * renewed[0]
        reactant = renewed[0] - absorbed
        product = renewed[1] + transfer(absorbed, frame_map, route_table, pick_slots, interp_weights)
        previous = current
        current = jnp.stack([reactant, product])
    return (previous, current)
```

```python
import functools

import jax
import jax.numpy as jnp
from jax import lax
from jax.experimental import pallas as pl
from jax.experimental.pallas import tpu as pltpu
from jax.sharding import PartitionSpec as P

JTOT = 23
HEL = 4
NA = 256
CR = 32
CS = 32
PTS = CR * CS
BLK = 8
NBLK = PTS // BLK
SRCS = 64
MSLOT = 4
TI = 8
ROWS = TI * CS
MIB = 1 << 20

kinetic = 0.08
rotor_scale = 0.1
centrifugal = 0.0005
coriolis_scale = 0.005
F32 = jnp.float32
BF16 = jnp.bfloat16
ALL = ("sec", "rr", "sr")


def dot(a, b):
    return jnp.dot(a, b, preferred_element_type=F32)


def split(x):
    high = x.astype(BF16)
    return high, (x - high.astype(F32)).astype(BF16)


def whole(shape, space=pltpu.VMEM):
    return pl.BlockSpec(shape, lambda *_: (0,) * len(shape), memory_space=space)


def smem():
    return pl.BlockSpec(memory_space=pltpu.SMEM)


def split_kernel(x_ref, high_ref, low_ref):
    high, low = split(x_ref[...])
    high_ref[...] = high
    low_ref[...] = low


def split_call(x, rows):
    total, width = x.shape
    spec = pl.BlockSpec((rows, width), lambda i: (i, 0))
    return pl.pallas_call(
        split_kernel,
        grid=(total // rows,),
        in_specs=[spec],
        out_specs=[spec, spec],
        out_shape=[jax.ShapeDtypeStruct(x.shape, BF16)] * 2,
        cost_estimate=pl.CostEstimate(flops=4 * x.size, transcendentals=0, bytes_accessed=8 * x.size),
        name="split_weights",
    )(x)


def blend_kernel(column_ref, live_ref, tile_ref, high_ref, low_ref, full):
    full[...] = jnp.zeros_like(full)
    lane_block = lax.broadcasted_iota(jnp.int32, (BLK, 128), 1) // BLK
    live = live_ref[0]

    def place(b, carry):
        row = pl.multiple_of(b * BLK, BLK)
        for m in range(MSLOT):
            column = column_ref[b * MSLOT + m]
            lane = pl.multiple_of((column // 16) * 128, 128)
            piece = jnp.where(lane_block == column % 16, tile_ref[b, m] * live, 0.0)
            full[pl.ds(row, BLK), pl.ds(lane, 128)] += piece
        return carry

    lax.fori_loop(0, NBLK, place, 0)

    def store(r, carry):
        row = pl.multiple_of(r * 64, 64)
        high, low = split(full[pl.ds(row, 64), :])
        high_ref[pl.ds(row, 64), :] = high
        low_ref[pl.ds(row, 64), :] = low
        return carry

    lax.fori_loop(0, PTS // 64, store, 0)


def blend_call(columns, live, tiles):
    return pl.pallas_call(
        blend_kernel,
        in_specs=[smem(), smem(), pl.BlockSpec(memory_space=pltpu.VMEM)],
        out_specs=[pl.BlockSpec(memory_space=pltpu.VMEM)] * 2,
        out_shape=[jax.ShapeDtypeStruct((PTS, PTS), BF16)] * 2,
        scratch_shapes=[pltpu.VMEM((PTS, PTS), F32)],
        compiler_params=pltpu.CompilerParams(vmem_limit_bytes=24 * MIB),
        cost_estimate=pl.CostEstimate(flops=8 * MIB, transcendentals=0, bytes_accessed=6 * MIB),
        name="blend_matrix",
    )(columns, live, tiles)


def step_kernel(want_own, want_pack, *refs):
    refs = list(refs)
    ids = refs.pop(0)
    u_ref, centre_ref, now, up, down, left, right, prev, pot, coef, w_high, w_low = refs[:12]
    refs = refs[12:]
    own_ref = refs.pop(0) if want_own else None
    pack_one, pack_zero = (refs.pop(0), refs.pop(0)) if want_pack else (None, None)
    rot, mix = refs.pop(0), refs.pop(0)
    absorbed = refs.pop(0) if want_pack else None
    chunk = pl.program_id(0)
    first = chunk * TI
    parts = [split(now[k, pl.ds(first, TI)].reshape(ROWS, NA)) for k in range(HEL)]

    def product(k, w):
        high, low = parts[k]
        return dot(high, w_high[w]) + dot(low, w_high[w]) + dot(high, w_low[w])

    for k in range(HEL):
        rot[k] = product(k, k)
        total = None
        if k < HEL - 1:
            total = product(k + 1, HEL + k)
        if k > 0:
            lower = product(k - 1, 2 * HEL - 2 + k)
            total = lower if total is None else total + lower
        mix[k] = total

    bond = lax.broadcasted_iota(jnp.int32, (CS, NA), 0)

    def row(t, carry):
        i = first + t
        u = u_ref[i]
        start = pl.multiple_of(t * CS, CS)
        damp, share, spin = (jnp.concatenate([coef[n, t]] * 2, axis=1) for n in range(3))
        well = pot[t] + 4.0 * kinetic
        for k in range(HEL):
            v = now[k, i]
            before = jnp.where(i == 0, up[k], now[k, jnp.maximum(i - 1, 0)])
            after = jnp.where(i == CR - 1, down[k], now[k, jnp.minimum(i + 1, CR - 1)])
            lower = jnp.where(bond == 0, left[k, pl.ds(i, 1), :], pltpu.roll(v, 1, 0))
            upper = jnp.where(bond == CS - 1, right[k, pl.ds(i, 1), :], pltpu.roll(v, CS - 1, 0))
            applied = (
                (well + u * centre_ref[k]) * v
                - kinetic * ((before + after) + (lower + upper))
                + spin * rot[k, pl.ds(start, CS), :]
                + u * mix[k, pl.ds(start, CS), :]
            )
            renewed = damp * (2.0 * applied - damp * prev[k, t])
            taken = share * renewed
            if want_own:
                own_ref[k, t] = renewed - taken
            if want_pack:
                absorbed[k, i] = taken
        return carry

    lax.fori_loop(0, TI, row, 0)

    if want_pack:

        @pl.when(chunk == CR // TI - 1)
        def _():
            def move(q, carry):
                for offset, target in ((0, pack_zero), (SRCS, pack_one)):
                    e = ids[offset + q]
                    i = e // (CS // BLK)
                    j = pl.multiple_of((e % (CS // BLK)) * BLK, BLK)
                    for k in range(HEL):
                        target[q, k] = absorbed[k, i, pl.ds(j, BLK), :]
                return carry

            lax.fori_loop(0, SRCS, move, 0)


def step_call(want_own, want_pack, ids, u, centre, now, halo, prev, pot, coef, w_high, w_low):
    field = (HEL, CR, CS, NA)
    rows = pl.BlockSpec((HEL, TI, CS, NA), lambda c: (0, c, 0, 0))
    out_specs, out_shape, scratch = [], [], []
    if want_own:
        out_specs.append(rows)
        out_shape.append(jax.ShapeDtypeStruct(field, F32))
    if want_pack:
        packed = (SRCS, HEL, BLK, NA)
        out_specs += [whole(packed)] * 2
        out_shape += [jax.ShapeDtypeStruct(packed, F32)] * 2
    scratch += [pltpu.VMEM((HEL, ROWS, NA), F32)] * 2
    if want_pack:
        scratch.append(pltpu.VMEM(field, F32))
    return pl.pallas_call(
        functools.partial(step_kernel, want_own, want_pack),
        grid=(CR // TI,),
        in_specs=[
            smem(),
            smem(),
            smem(),
            whole(field),
            whole((HEL, CS, NA)),
            whole((HEL, CS, NA)),
            whole((HEL, CR, NA)),
            whole((HEL, CR, NA)),
            rows,
            pl.BlockSpec((TI, CS, NA), lambda c: (c, 0, 0)),
            pl.BlockSpec((3, TI, CS, 128), lambda c: (0, c, 0, 0)),
            whole((10, NA, NA)),
            whole((10, NA, NA)),
        ],
        out_specs=out_specs,
        out_shape=out_shape,
        scratch_shapes=scratch,
        compiler_params=pltpu.CompilerParams(vmem_limit_bytes=48 * MIB),
        cost_estimate=pl.CostEstimate(flops=30 * 2 * PTS * NA * NA, transcendentals=0, bytes_accessed=20 * MIB),
        name="step_own" if want_own and not want_pack else "step_pack" if not want_own else "step_both",
    )(ids, u, centre, now, *halo, prev, pot, coef, w_high, w_low)


def inflow_kernel(x_ref, f_high, f_low, b_high, b_low, acc_ref, out_ref, x_high, x_low):
    half = SRCS * BLK

    @pl.when(pl.program_id(0) == 0)
    def _():
        for k in range(HEL):
            high, low = split(x_ref[:, k].reshape(half, NA))
            x_high[k] = high
            x_low[k] = low

    framed = None
    for k in range(HEL):
        rows = slice(k * NA, (k + 1) * NA)
        term = dot(x_high[k], f_high[rows]) + dot(x_low[k], f_high[rows]) + dot(x_high[k], f_low[rows])
        framed = term if framed is None else framed + term
    high, low = split(framed)
    for r in range(4):
        rows = slice(r * PTS // 4, (r + 1) * PTS // 4)
        out_ref[0, rows] = acc_ref[0, rows] + (dot(b_high[rows], high) + dot(b_low[rows], high) + dot(b_high[rows], low))


def inflow_call(part, x, frame, blend, acc):
    half = SRCS * BLK
    column = pl.BlockSpec((HEL * NA, NA), lambda n: (0, n))
    weights = pl.BlockSpec((PTS, half), lambda n: (0, part))
    field = pl.BlockSpec((1, PTS, NA), lambda n: (n, 0, 0))
    return pl.pallas_call(
        inflow_kernel,
        grid=(HEL,),
        in_specs=[whole((SRCS, HEL, BLK, NA)), column, column, weights, weights, field],
        out_specs=field,
        out_shape=jax.ShapeDtypeStruct((HEL, PTS, NA), F32),
        scratch_shapes=[pltpu.VMEM((HEL, half, NA), BF16)] * 2,
        compiler_params=pltpu.CompilerParams(vmem_limit_bytes=40 * MIB),
        cost_estimate=pl.CostEstimate(flops=12 * half * PTS * PTS, transcendentals=0, bytes_accessed=16 * MIB),
        name="inflow",
    )(x, *frame, *blend, acc)


def edges(x):
    rows, columns = lax.axis_size("rr"), lax.axis_size("sr")

    def send(piece, axis, peers, forward):
        pairs = [(i, i + 1) if forward else (i + 1, i) for i in range(peers - 1)]
        return lax.ppermute(piece, axis, pairs)

    return (
        send(x[:, CR - 1], "rr", rows, True),
        send(x[:, 0], "rr", rows, False),
        send(x[:, :, CS - 1], "sr", columns, True),
        send(x[:, :, 0], "sr", columns, False),
    )


def cross(x):
    pairs = [(s, SRCS + (s ^ (SRCS // 2))) for s in range(SRCS)]
    return lax.ppermute(x, ALL, pairs)


def spread(x):
    return lax.all_to_all(x, ("rr", "sr"), split_axis=0, concat_axis=0, tiled=True)


def per_device(
    wave_prev,
    wave_now,
    potential,
    damping,
    switch,
    angular,
    coriolis,
    helicity_start,
    frame_map,
    route_table,
    pick_slots,
    interp_weights,
):
    section = lax.axis_index("sec")
    row_slab = lax.axis_index("rr")
    col_slab = lax.axis_index("sr")
    previous, current, pot = wave_prev[0], wave_now[0], potential[0]
    halo = edges(current)

    radial_pos = (row_slab * CR + jnp.arange(CR)).astype(F32)
    bond_pos = (col_slab * CS + jnp.arange(CS)).astype(F32)
    radial = (1.0 + 3.0 * radial_pos / float(lax.axis_size("rr") * CR)) ** (-2)
    bond = (1.0 + 3.0 * bond_pos / float(lax.axis_size("sr") * CS)) ** (-2)
    helicity = helicity_start[0].astype(F32) + jnp.arange(HEL, dtype=F32)
    total_j = float(JTOT * (JTOT + 1))
    ladder = coriolis_scale * jnp.sqrt(total_j - helicity * (helicity + 1.0))[:-1, None, None]
    centre = centrifugal * (total_j - 2.0 * helicity * helicity)
    coef = jnp.stack(
        [
            damping[0],
            jnp.where(section == 0, switch, 0.0),
            rotor_scale * (radial[:, None] + bond[None, :]),
        ]
    )
    coef = jnp.broadcast_to(coef[..., None], (3, CR, CS, 128))
    weights = jnp.concatenate(
        [jnp.swapaxes(angular[0], 1, 2), ladder * jnp.swapaxes(coriolis[0], 1, 2), ladder * coriolis[0]], 0
    )
    w_high, w_low = (w.reshape(10, NA, NA) for w in split_call(weights.reshape(10 * NA, NA), NA))

    me = row_slab * lax.axis_size("sr") + col_slab
    outgoing = jnp.maximum(lax.dynamic_index_in_dim(route_table, me, axis=1, keepdims=False), 0)
    flip = jnp.arange(SRCS) ^ (SRCS // 2)
    ids = jnp.concatenate([outgoing[flip, 0], outgoing[:, 1]])

    picks = pick_slots[0, 0].reshape(NBLK * MSLOT)
    source, slot = picks // 2, picks % 2
    columns = jnp.where(slot == 0, source, SRCS + (source ^ (SRCS // 2)))
    live = (section == 1).astype(F32).reshape(1)
    blend = blend_call(columns, live, jnp.tile(interp_weights[0, 0], (1, 1, 1, 128 // BLK)))
    frame = split_call(frame_map.reshape(HEL * NA, HEL * NA), NA)

    fixed = (pot, coef, w_high, w_low)
    field = (HEL, CR, CS, NA)
    flat = (HEL, PTS, NA)

    own_1, one_1, zero_1 = step_call(True, True, ids, radial, centre, current, halo, previous, *fixed)
    crossed_one_1 = cross(one_1)
    relayed_1 = spread(zero_1)
    crossed_zero_1 = cross(relayed_1)
    one_2, zero_2 = step_call(False, True, ids, radial, centre, own_1, edges(own_1), current, *fixed)
    crossed_one_2 = cross(one_2)
    shared = spread(jnp.where(section == 0, zero_2, crossed_one_1))
    crossed_zero_2 = cross(shared)

    new_1 = inflow_call(1, shared, frame, blend, own_1.reshape(flat))
    new_1 = inflow_call(0, crossed_zero_1, frame, blend, new_1).reshape(field)
    (own_2,) = step_call(True, False, ids, radial, centre, new_1, edges(new_1), current, *fixed)

    last_one = spread(crossed_one_2)
    new_2 = inflow_call(1, last_one, frame, blend, own_2.reshape(flat))
    new_2 = inflow_call(0, crossed_zero_2, frame, blend, new_2).reshape(field)
    return new_1[None], new_2[None]


def solution(mesh):
    placed = (
        P("sec", None, "rr", "sr", None),
        P("sec", None, "rr", "sr", None),
        P("sec", "rr", "sr", None),
        P("sec", "rr", "sr"),
        P("rr", "sr"),
        P("sec", None, None, None),
        P("sec", None, None, None),
        P("sec"),
        P(),
        P(),
        P("rr", "sr", None, None),
        P("rr", "sr", None, None, None, None),
    )
    return jax.shard_map(
        per_device,
        mesh=mesh,
        in_specs=placed,
        out_specs=(P("sec", None, "rr", "sr", None), P("sec", None, "rr", "sr", None)),
        check_vma=False,
    )
```

```python
import functools

import jax
import jax.numpy as jnp
from jax import lax
from jax.experimental import pallas as pl
from jax.experimental.pallas import tpu as pltpu
from jax.sharding import PartitionSpec as P

JTOT = 23
HEL = 4
NA = 256
CR = 32
CS = 32
PTS = CR * CS
BLK = 8
NBLK = PTS // BLK
SRCS = 64
MSLOT = 4
TI = 8
ROWS = TI * CS
MIB = 1 << 20

kinetic = 0.08
rotor_scale = 0.1
centrifugal = 0.0005
coriolis_scale = 0.005
F32 = jnp.float32
BF16 = jnp.bfloat16
ALL = ("sec", "rr", "sr")


def dot(a, b):
    return jnp.dot(a, b, preferred_element_type=F32)


def split(x):
    high = x.astype(BF16)
    return high, (x - high.astype(F32)).astype(BF16)


def whole(shape, space=pltpu.VMEM):
    return pl.BlockSpec(shape, lambda *_: (0,) * len(shape), memory_space=space)


def smem():
    return pl.BlockSpec(memory_space=pltpu.SMEM)


def frame_terms(frame_map):
    turned = frame_map.transpose(2, 0, 1, 3).reshape(HEL, HEL * NA, NA)
    high = lax.reduce_precision(turned, 8, 7)
    return high.astype(BF16), (turned - high).astype(BF16)


def blend_kernel(pick_ref, tile_ref, high_ref, low_ref, full):
    full[...] = jnp.zeros_like(full)
    lane_block = lax.broadcasted_iota(jnp.int32, (BLK, 128), 1) // BLK

    def place(b, carry):
        row = pl.multiple_of(b * BLK, BLK)
        for m in range(MSLOT):
            pick = pick_ref[m * NBLK + b]
            source, slot = pick // 2, pick % 2
            column = jnp.where(slot == 0, source, SRCS + (source ^ (SRCS // 2)))
            lane = pl.multiple_of((column // 16) * 128, 128)
            piece = jnp.where(lane_block == column % 16, tile_ref[b, m], 0.0)
            full[pl.ds(row, BLK), pl.ds(lane, 128)] += piece
        return carry

    lax.fori_loop(0, NBLK, place, 0)

    def store(r, carry):
        row = pl.multiple_of(r * 64, 64)
        high, low = split(full[pl.ds(row, 64), :])
        high_ref[pl.ds(row, 64), :] = high
        low_ref[pl.ds(row, 64), :] = low
        return carry

    lax.fori_loop(0, PTS // 64, store, 0)


def blend_call(picks, tiles):
    return pl.pallas_call(
        blend_kernel,
        in_specs=[smem(), pl.BlockSpec(memory_space=pltpu.VMEM)],
        out_specs=[pl.BlockSpec(memory_space=pltpu.VMEM)] * 2,
        out_shape=[jax.ShapeDtypeStruct((PTS, PTS), BF16)] * 2,
        scratch_shapes=[pltpu.VMEM((PTS, PTS), F32)],
        compiler_params=pltpu.CompilerParams(vmem_limit_bytes=24 * MIB),
        cost_estimate=pl.CostEstimate(flops=8 * MIB, transcendentals=0, bytes_accessed=6 * MIB),
        name="blend_matrix",
    )(picks, tiles)


ABOVE = (4, 5, 7)
BELOW = (6, 8, 9)


def step_kernel(first_step, want_own, want_pack, *refs):
    refs = list(refs)
    ids = refs.pop(0) if want_pack else None
    start_ref, now, up, down, left, right, prev, pot, damping, switch = refs[:10]
    refs = refs[10:]
    if first_step:
        angular, coriolis = refs.pop(0), refs.pop(0)
    else:
        w_ref = refs.pop(0)
    own_ref = refs.pop(0) if want_own else None
    if want_pack:
        pack_one, pack_zero = refs.pop(0), refs.pop(0)
    if first_step:
        top_ref, bottom_ref, left_ref, right_ref, w_ref = refs[:5]
        refs = refs[5:]
    rot, mix = refs.pop(0), refs.pop(0)
    absorbed = refs.pop(0) if want_pack else None
    chunk = pl.program_id(0)
    first = chunk * TI
    lowest = start_ref[0]
    total_j = float(JTOT * (JTOT + 1))

    if first_step:

        @pl.when(chunk == 0)
        def _():
            def put(n, w):
                high, low = split(w)
                w_ref[n, 0:NA] = high
                w_ref[n, NA : 2 * NA] = high
                w_ref[n, 2 * NA : 3 * NA] = low

            for k in range(HEL):
                put(k, angular[k].T)
            for k in range(HEL - 1):
                helicity = (lowest + k).astype(F32)
                ladder = coriolis_scale * jnp.sqrt(jnp.full((NA, NA), total_j - helicity * (helicity + 1.0), F32))
                scaled = ladder * coriolis[k]
                put(ABOVE[k], scaled.T)
                put(BELOW[k], scaled)

    parts = []
    for k in range(HEL):
        high, low = split(now[k, pl.ds(first, TI)].reshape(ROWS, NA))
        parts.append(jnp.concatenate([high, low, high], axis=1))
    for k in range(HEL):
        rot[k] = dot(parts[k], w_ref[k])
    mix[0] = dot(parts[1], w_ref[ABOVE[0]])
    for k in (1, 2):
        both = jnp.concatenate([parts[k + 1], parts[k - 1]], axis=1)
        mix[k] = dot(both, w_ref[ABOVE[k] : ABOVE[k] + 2].reshape(6 * NA, NA))
    mix[3] = dot(parts[2], w_ref[BELOW[2]])

    bond = lax.broadcasted_iota(jnp.int32, (CS, NA), 0)
    diagonal = lax.broadcasted_iota(jnp.int32, (CS, CS), 0) == lax.broadcasted_iota(jnp.int32, (CS, CS), 1)
    live = jnp.where(lax.axis_index("sec") == 0, 1.0, 0.0)

    def factor(position, cells):
        base = 1.0 + 3.0 * position.astype(F32) / float(cells)
        return 1.0 / (base * base)

    bond_cells = lax.axis_size("sr") * CS
    bond_factor = factor(lax.axis_index("sr") * CS + bond, bond_cells)
    radial_cells = lax.axis_size("rr") * CR
    radial_start = lax.axis_index("rr") * CR + first
    helicities = [(lowest + k).astype(F32) for k in range(HEL)]
    centre = [centrifugal * (total_j - 2.0 * h * h) for h in helicities]

    def column(ref, i):
        line = jnp.broadcast_to(ref[pl.ds(i, 1), :], (CS, CS))
        return jnp.sum(jnp.where(diagonal, line, 0.0), axis=1, keepdims=True)

    def row(t, carry):
        i = first + t
        u = factor(jnp.full((CS, NA), radial_start + t, jnp.int32), radial_cells)
        start = pl.multiple_of(t * CS, CS)
        damp = jnp.broadcast_to(column(damping, i), (CS, NA))
        share = jnp.broadcast_to(column(switch, i) * live, (CS, NA))
        spin = rotor_scale * (u + bond_factor)
        well = pot[t] + 4.0 * kinetic
        for k in range(HEL):
            v = now[k, i]
            before = jnp.where(i == 0, up[k], now[k, jnp.maximum(i - 1, 0)])
            after = jnp.where(i == CR - 1, down[k], now[k, jnp.minimum(i + 1, CR - 1)])
            lower = jnp.where(bond == 0, left[k, pl.ds(i, 1), :], pltpu.roll(v, 1, 0))
            upper = jnp.where(bond == CS - 1, right[k, pl.ds(i, 1), :], pltpu.roll(v, CS - 1, 0))
            applied = (
                (well + u * centre[k]) * v
                - kinetic * ((before + after) + (lower + upper))
                + spin * rot[k, pl.ds(start, CS), :]
                + u * mix[k, pl.ds(start, CS), :]
            )
            renewed = damp * (2.0 * applied - damp * prev[k, t])
            taken = share * renewed
            if want_own:
                own_ref[k, t] = renewed - taken
            if want_pack:
                absorbed[k, i] = taken
        return carry

    lax.fori_loop(0, TI, row, 0)

    if first_step:
        for k in range(HEL):
            left_ref[k, pl.ds(pl.multiple_of(first, TI), TI), :] = own_ref[k, :, 0, :]
            right_ref[k, pl.ds(pl.multiple_of(first, TI), TI), :] = own_ref[k, :, CS - 1, :]

        @pl.when(chunk == 0)
        def _():
            top_ref[...] = own_ref[:, 0]

        @pl.when(chunk == CR // TI - 1)
        def _():
            bottom_ref[...] = own_ref[:, TI - 1]

    if want_pack:

        @pl.when(chunk == CR // TI - 1)
        def _():
            def move(q, carry):
                for slot, target in ((q ^ (SRCS // 2), pack_zero), (SRCS + (q if first_step else q ^ (SRCS // 2)), pack_one)):
                    e = jnp.maximum(ids[slot], 0)
                    i = e // (CS // BLK)
                    j = pl.multiple_of((e % (CS // BLK)) * BLK, BLK)
                    for k in range(HEL):
                        target[q, k] = absorbed[k, i, pl.ds(j, BLK), :]
                return carry

            lax.fori_loop(0, SRCS, move, 0)


def step_call(first_step, want_own, want_pack, ids, helicity_start, now, halo, prev, pot, damping, switch, *weights):
    field = (HEL, CR, CS, NA)
    edge = (HEL, CR, NA)
    stack = (10, 3 * NA, NA)
    rows = pl.BlockSpec((HEL, TI, CS, NA), lambda c: (0, c, 0, 0))
    out_specs, out_shape, scratch = [], [], []
    if want_own:
        out_specs.append(rows)
        out_shape.append(jax.ShapeDtypeStruct(field, F32))
    if want_pack:
        packed = (SRCS, HEL, BLK, NA)
        out_specs += [whole(packed)] * 2
        out_shape += [jax.ShapeDtypeStruct(packed, F32)] * 2
    if first_step:
        out_specs += [whole(edge)] * 4 + [whole(stack)]
        out_shape += [jax.ShapeDtypeStruct(edge, F32)] * 4 + [jax.ShapeDtypeStruct(stack, BF16)]
    scratch += [pltpu.VMEM((HEL, ROWS, NA), F32)] * 2
    if want_pack:
        scratch.append(pltpu.VMEM(field, F32))
    weight_specs = [whole((HEL, NA, NA)), whole((HEL - 1, NA, NA))] if first_step else [whole(stack)]
    return pl.pallas_call(
        functools.partial(step_kernel, first_step, want_own, want_pack),
        grid=(CR // TI,),
        in_specs=([smem()] if want_pack else [])
        + [
            smem(),
            whole(field),
            whole(edge),
            whole(edge),
            whole(edge),
            whole(edge),
            rows,
            pl.BlockSpec((TI, CS, NA), lambda c: (c, 0, 0)),
            whole((CR, CS)),
            whole((CR, CS)),
        ]
        + weight_specs,
        out_specs=out_specs,
        out_shape=out_shape,
        scratch_shapes=scratch,
        compiler_params=pltpu.CompilerParams(vmem_limit_bytes=56 * MIB),
        cost_estimate=pl.CostEstimate(flops=1000, transcendentals=0, bytes_accessed=1000),
        name="step_first" if first_step else "step_own" if want_own else "step_pack",
    )(*((ids,) if want_pack else ()), helicity_start, now, *halo, prev, pot, damping, switch, *weights)


def inflow_kernel(want_edges, swap, x_ref, f_high, f_low, b_high, b_low, acc_ref, *refs):
    half = SRCS * BLK
    out_ref = refs[0]
    terms = refs[-1]
    product_section = lax.axis_index("sec") == 1

    @pl.when(jnp.logical_and(product_section, pl.program_id(0) == 0))
    def _():
        for k in range(HEL):
            lanes = slice(k * NA, (k + 1) * NA)
            for part in range(2):
                source = (1 - part if swap else part) * (SRCS // 2)
                row = part * half // 2
                high, low = split(x_ref[source : source + SRCS // 2, k].reshape(half // 2, NA))
                terms[row : row + half // 2, lanes] = high
                terms[half + row : half + row + half // 2, lanes] = low

    @pl.when(product_section)
    def _():
        wide = dot(terms[...], f_high[0])
        high, low = split(wide[:half] + wide[half:] + dot(terms[0:half], f_low[0]))
        for r in range(2):
            rows = slice(r * PTS // 2, (r + 1) * PTS // 2)
            gain = dot(b_high[rows], high) + dot(b_low[rows], high) + dot(b_high[rows], low)
            lines = slice(r * CR // 2, (r + 1) * CR // 2)
            out_ref[0, lines] = acc_ref[0, lines] + gain.reshape(CR // 2, CS, NA)

    @pl.when(jnp.logical_not(product_section))
    def _():
        out_ref[...] = acc_ref[...]

    if want_edges:
        top_ref, bottom_ref, left_ref, right_ref = refs[1:5]
        top_ref[0] = out_ref[0, 0]
        bottom_ref[0] = out_ref[0, CR - 1]
        left_ref[0] = out_ref[0, :, 0, :]
        right_ref[0] = out_ref[0, :, CS - 1, :]


def inflow_call(part, want_edges, swap, x, frame, blend, acc, flops=1000):
    half = SRCS * BLK
    column = pl.BlockSpec((1, HEL * NA, NA), lambda n: (n, 0, 0))
    weights = pl.BlockSpec((PTS, half), lambda n: (0, part))
    field = pl.BlockSpec((1, CR, CS, NA), lambda n: (n, 0, 0, 0))
    edge = pl.BlockSpec((1, CR, NA), lambda n: (n, 0, 0))
    count = 4 if want_edges else 0
    return pl.pallas_call(
        functools.partial(inflow_kernel, want_edges, swap),
        grid=(HEL,),
        in_specs=[whole((SRCS, HEL, BLK, NA)), column, column, weights, weights, field],
        out_specs=[field] + [edge] * count,
        out_shape=[jax.ShapeDtypeStruct((HEL, CR, CS, NA), F32)] + [jax.ShapeDtypeStruct((HEL, CR, NA), F32)] * count,
        scratch_shapes=[pltpu.VMEM((2 * half, HEL * NA), BF16)],
        compiler_params=pltpu.CompilerParams(vmem_limit_bytes=56 * MIB),
        cost_estimate=pl.CostEstimate(flops=flops, transcendentals=0, bytes_accessed=1000),
        name="inflow_edges" if want_edges else "inflow",
    )(x, *frame, *blend, acc)


def exchange(top, bottom, left, right):
    rows, columns = lax.axis_size("rr"), lax.axis_size("sr")

    def send(piece, axis, peers, forward):
        pairs = [(i, i + 1) if forward else (i + 1, i) for i in range(peers - 1)]
        return lax.ppermute(piece, axis, pairs)

    return (
        send(bottom, "rr", rows, True),
        send(top, "rr", rows, False),
        send(right, "sr", columns, True),
        send(left, "sr", columns, False),
    )


def cross(x):
    pairs = [(s, SRCS + (s ^ (SRCS // 2))) for s in range(SRCS)]
    return lax.ppermute(x, ALL, pairs)


def spread(x):
    return lax.all_to_all(x, ("rr", "sr"), split_axis=0, concat_axis=0, tiled=True)


def per_device(
    wave_prev,
    wave_now,
    potential,
    damping,
    switch,
    angular,
    coriolis,
    helicity_start,
    frame_map,
    route_table,
    pick_slots,
    interp_weights,
):
    section = lax.axis_index("sec")
    me = lax.axis_index("rr") * lax.axis_size("sr") + lax.axis_index("sr")
    previous, current = wave_prev[0], wave_now[0]
    halo = exchange(current[:, 0], current[:, CR - 1], current[:, :, 0], current[:, :, CS - 1])
    outgoing = lax.dynamic_index_in_dim(route_table, me, axis=1, keepdims=False)
    ids = outgoing.T.reshape(2 * SRCS)

    fixed = (potential[0], damping[0], switch)

    own_1, one_1, zero_1, *rims, weights = step_call(
        True, True, True, ids, helicity_start, current, halo, previous, *fixed, angular[0], coriolis[0]
    )
    crossed_one_1 = cross(one_1)
    halo = exchange(*rims)
    zero_1, halo = lax.optimization_barrier((zero_1, halo))
    relayed_1 = spread(zero_1)
    packed = (SRCS, HEL, BLK, NA)

    def reactant(own, halo, weights, *_):
        one, zero = step_call(False, False, True, ids, helicity_start, own, halo, current, *fixed, weights)
        return one, zero, (jnp.zeros((PTS, PTS), BF16),) * 2, (jnp.zeros((HEL, HEL * NA, NA), BF16),) * 2

    def product(own, halo, weights, picks, tiles, frame_map):
        blend = blend_call(picks, jnp.tile(tiles, (1, 1, 1, 128 // BLK)))
        return jnp.zeros(packed, F32), jnp.zeros(packed, F32), tuple(blend), frame_terms(frame_map)

    picks = pick_slots[0, 0].T.reshape(MSLOT * NBLK)
    one_2, zero_2, blend, frame = lax.cond(
        section == 0, reactant, product, own_1, halo, weights, picks, interp_weights[0, 0], frame_map
    )
    crossed_zero_1 = cross(relayed_1)
    shared = spread(jnp.where(section == 0, zero_2, crossed_one_1))
    crossed_zero_2 = cross(shared)
    one_2, shared = lax.optimization_barrier((one_2, shared))
    relayed_2 = spread(one_2)

    (new_1,) = inflow_call(0, False, False, crossed_zero_1, frame, blend, own_1, 40 << 30)
    new_1, *rims = inflow_call(1, True, False, shared, frame, blend, new_1)
    relayed_2, rims = lax.optimization_barrier((relayed_2, rims))
    crossed_one_2 = cross(relayed_2)
    halo = exchange(*rims)
    (own_2,) = step_call(False, True, False, ids, helicity_start, new_1, halo, current, *fixed, weights)
    (new_2,) = inflow_call(0, False, False, crossed_zero_2, frame, blend, own_2)
    (new_2,) = inflow_call(1, False, True, crossed_one_2, frame, blend, new_2)
    return new_1[None], new_2[None]


def solution(mesh):
    placed = (
        P("sec", None, "rr", "sr", None),
        P("sec", None, "rr", "sr", None),
        P("sec", "rr", "sr", None),
        P("sec", "rr", "sr"),
        P("rr", "sr"),
        P("sec", None, None, None),
        P("sec", None, None, None),
        P("sec"),
        P(),
        P(),
        P("rr", "sr", None, None),
        P("rr", "sr", None, None, None, None),
    )
    return jax.shard_map(
        per_device,
        mesh=mesh,
        in_specs=placed,
        out_specs=(P("sec", None, "rr", "sr", None), P("sec", None, "rr", "sr", None)),
        check_vma=False,
    )
```

```python
import functools

import jax
import jax.numpy as jnp
from jax import lax
from jax.experimental import pallas as pl
from jax.experimental.pallas import tpu as pltpu
from jax.sharding import PartitionSpec as P

JTOT = 23
HEL = 4
NA = 256
CR = 32
CS = 32
PTS = CR * CS
BLK = 8
NBLK = PTS // BLK
SRCS = 64
MSLOT = 4
TI = 8
ROWS = TI * CS
MIB = 1 << 20

kinetic = 0.08
rotor_scale = 0.1
centrifugal = 0.0005
coriolis_scale = 0.005
F32 = jnp.float32
BF16 = jnp.bfloat16
ALL = ("sec", "rr", "sr")


def dot(a, b):
    return jnp.dot(a, b, preferred_element_type=F32)


def split(x):
    high = x.astype(BF16)
    return high, (x - high.astype(F32)).astype(BF16)


def whole(shape, space=pltpu.VMEM):
    return pl.BlockSpec(shape, lambda *_: (0,) * len(shape), memory_space=space)


def smem():
    return pl.BlockSpec(memory_space=pltpu.SMEM)


def frame_terms(frame_map):
    turned = frame_map.transpose(2, 0, 1, 3).reshape(HEL, HEL * NA, NA)
    high = lax.reduce_precision(turned, 8, 7)
    return high.astype(BF16), (turned - high).astype(BF16)


def blend_kernel(pick_ref, tile_ref, high_ref, low_ref, *unused):
    lane_block = lax.broadcasted_iota(jnp.int32, (BLK, PTS), 1) // BLK

    def rows_of(b):
        total = None
        for m in range(MSLOT):
            pick = pick_ref[m * NBLK + b]
            source, slot = pick // 2, pick % 2
            column = jnp.where(slot == 0, source, SRCS + (source ^ (SRCS // 2)))
            spread_tile = jnp.concatenate([tile_ref[b, m]] * (PTS // 128), axis=1)
            piece = jnp.where(lane_block == column, spread_tile, 0.0)
            total = piece if total is None else total + piece
        return total

    def pair(n, carry):
        row = pl.multiple_of(n * 2 * BLK, 2 * BLK)
        high, low = split(jnp.concatenate([rows_of(2 * n), rows_of(2 * n + 1)], axis=0))
        high_ref[pl.ds(row, 2 * BLK), :] = high
        low_ref[pl.ds(row, 2 * BLK), :] = low
        return carry

    lax.fori_loop(0, NBLK // 2, pair, 0)


def untouched(shapes):
    return [pl.BlockSpec(memory_space=pl.ANY)] * len(shapes), list(shapes)


def blend_call(picks, tiles, others):
    specs, shapes = untouched(others)
    return pl.pallas_call(
        blend_kernel,
        in_specs=[smem(), pl.BlockSpec(memory_space=pltpu.VMEM)],
        out_specs=[pl.BlockSpec(memory_space=pltpu.VMEM)] * 2 + specs,
        out_shape=[jax.ShapeDtypeStruct((PTS, PTS), BF16)] * 2 + shapes,
        compiler_params=pltpu.CompilerParams(vmem_limit_bytes=24 * MIB),
        cost_estimate=pl.CostEstimate(flops=8 * MIB, transcendentals=0, bytes_accessed=6 * MIB),
        name="blend_matrix",
    )(picks, tiles)


ABOVE = (4, 5, 7)
BELOW = (6, 8, 9)


def step_kernel(first_step, want_own, want_pack, *refs):
    refs = list(refs)
    ids = refs.pop(0) if want_pack else None
    start_ref, now, up, down, left, right, prev, pot, damping, switch = refs[:10]
    refs = refs[10:]
    if first_step:
        angular, coriolis = refs.pop(0), refs.pop(0)
    else:
        w_ref = refs.pop(0)
    own_ref = refs.pop(0) if want_own else None
    if want_pack:
        pack_one, pack_zero = refs.pop(0), refs.pop(0)
    if first_step:
        top_ref, bottom_ref, left_ref, right_ref, w_ref = refs[:5]
        refs = refs[5:]
    rot, mix = refs[-3:-1] if want_pack else refs[-2:]
    absorbed = refs[-1] if want_pack else None
    chunk = pl.program_id(0)
    first = chunk * TI
    lowest = start_ref[0]
    total_j = float(JTOT * (JTOT + 1))

    if first_step:

        @pl.when(chunk == 0)
        def _():
            def put(n, w):
                high, low = split(w)
                w_ref[n, 0:NA] = high
                w_ref[n, NA : 2 * NA] = high
                w_ref[n, 2 * NA : 3 * NA] = low

            for k in range(HEL):
                put(k, angular[k].T)
            for k in range(HEL - 1):
                helicity = (lowest + k).astype(F32)
                ladder = coriolis_scale * jnp.sqrt(jnp.full((NA, NA), total_j - helicity * (helicity + 1.0), F32))
                scaled = ladder * coriolis[k]
                put(ABOVE[k], scaled.T)
                put(BELOW[k], scaled)

    parts = []
    for k in range(HEL):
        high, low = split(now[k, pl.ds(first, TI)].reshape(ROWS, NA))
        parts.append(jnp.concatenate([high, low, high], axis=1))
    for k in range(HEL):
        rot[k] = dot(parts[k], w_ref[k])
    mix[0] = dot(parts[1], w_ref[ABOVE[0]])
    for k in (1, 2):
        both = jnp.concatenate([parts[k + 1], parts[k - 1]], axis=1)
        mix[k] = dot(both, w_ref[ABOVE[k] : ABOVE[k] + 2].reshape(6 * NA, NA))
    mix[3] = dot(parts[2], w_ref[BELOW[2]])

    bond = lax.broadcasted_iota(jnp.int32, (CS, NA), 0)
    diagonal = lax.broadcasted_iota(jnp.int32, (CS, CS), 0) == lax.broadcasted_iota(jnp.int32, (CS, CS), 1)
    live = jnp.where(lax.axis_index("sec") == 0, 1.0, 0.0)

    def factor(position, cells):
        base = 1.0 + 3.0 * position.astype(F32) / float(cells)
        return 1.0 / (base * base)

    bond_cells = lax.axis_size("sr") * CS
    bond_factor = factor(lax.axis_index("sr") * CS + bond, bond_cells)
    radial_cells = lax.axis_size("rr") * CR
    radial_start = lax.axis_index("rr") * CR + first
    helicities = [(lowest + k).astype(F32) for k in range(HEL)]
    centre = [centrifugal * (total_j - 2.0 * h * h) for h in helicities]

    def column(ref, i):
        line = jnp.broadcast_to(ref[pl.ds(i, 1), :], (CS, CS))
        return jnp.sum(jnp.where(diagonal, line, 0.0), axis=1, keepdims=True)

    def row(t, carry):
        i = first + t
        u = factor(jnp.full((CS, NA), radial_start + t, jnp.int32), radial_cells)
        start = pl.multiple_of(t * CS, CS)
        damp = jnp.broadcast_to(column(damping, i), (CS, NA))
        share = jnp.broadcast_to(column(switch, i) * live, (CS, NA))
        spin = rotor_scale * (u + bond_factor)
        well = pot[t] + 4.0 * kinetic
        for k in range(HEL):
            v = now[k, i]
            before = jnp.where(i == 0, up[k], now[k, jnp.maximum(i - 1, 0)])
            after = jnp.where(i == CR - 1, down[k], now[k, jnp.minimum(i + 1, CR - 1)])
            lower = jnp.where(bond == 0, left[k, pl.ds(i, 1), :], pltpu.roll(v, 1, 0))
            upper = jnp.where(bond == CS - 1, right[k, pl.ds(i, 1), :], pltpu.roll(v, CS - 1, 0))
            applied = (
                (well + u * centre[k]) * v
                - kinetic * ((before + after) + (lower + upper))
                + spin * rot[k, pl.ds(start, CS), :]
                + u * mix[k, pl.ds(start, CS), :]
            )
            renewed = damp * (2.0 * applied - damp * prev[k, t])
            taken = share * renewed
            if want_own:
                own_ref[k, t] = renewed - taken
            if want_pack:
                absorbed[k, i] = taken
        return carry

    lax.fori_loop(0, TI, row, 0)

    if first_step:
        for k in range(HEL):
            left_ref[k, pl.ds(pl.multiple_of(first, TI), TI), :] = own_ref[k, :, 0, :]
            right_ref[k, pl.ds(pl.multiple_of(first, TI), TI), :] = own_ref[k, :, CS - 1, :]

        @pl.when(chunk == 0)
        def _():
            top_ref[...] = own_ref[:, 0]

        @pl.when(chunk == CR // TI - 1)
        def _():
            bottom_ref[...] = own_ref[:, TI - 1]

    if want_pack:

        @pl.when(chunk == CR // TI - 1)
        def _():
            def move(q, carry):
                for slot, target in ((q ^ (SRCS // 2), pack_zero), (SRCS + (q if first_step else q ^ (SRCS // 2)), pack_one)):
                    e = jnp.maximum(ids[slot], 0)
                    i = e // (CS // BLK)
                    j = pl.multiple_of((e % (CS // BLK)) * BLK, BLK)
                    for k in range(HEL):
                        target[q, k] = absorbed[k, i, pl.ds(j, BLK), :]
                return carry

            lax.fori_loop(0, SRCS, move, 0)


def step_call(first_step, want_own, want_pack, ids, helicity_start, now, halo, prev, pot, damping, switch, *weights, others=()):
    field = (HEL, CR, CS, NA)
    edge = (HEL, CR, NA)
    stack = (10, 3 * NA, NA)
    rows = pl.BlockSpec((HEL, TI, CS, NA), lambda c: (0, c, 0, 0))
    out_specs, out_shape, scratch = [], [], []
    if want_own:
        out_specs.append(rows)
        out_shape.append(jax.ShapeDtypeStruct(field, F32))
    if want_pack:
        packed = (SRCS, HEL, BLK, NA)
        out_specs += [whole(packed)] * 2
        out_shape += [jax.ShapeDtypeStruct(packed, F32)] * 2
    if first_step:
        out_specs += [whole(edge)] * 4 + [whole(stack)]
        out_shape += [jax.ShapeDtypeStruct(edge, F32)] * 4 + [jax.ShapeDtypeStruct(stack, BF16)]
    specs, shapes = untouched(others)
    out_specs += specs
    out_shape += shapes
    scratch += [pltpu.VMEM((HEL, ROWS, NA), F32)] * 2
    if want_pack:
        scratch.append(pltpu.VMEM(field, F32))
    weight_specs = [whole((HEL, NA, NA)), whole((HEL - 1, NA, NA))] if first_step else [whole(stack)]
    return pl.pallas_call(
        functools.partial(step_kernel, first_step, want_own, want_pack),
        grid=(CR // TI,),
        in_specs=([smem()] if want_pack else [])
        + [
            smem(),
            whole(field),
            whole(edge),
            whole(edge),
            whole(edge),
            whole(edge),
            rows,
            pl.BlockSpec((TI, CS, NA), lambda c: (c, 0, 0)),
            whole((CR, CS)),
            whole((CR, CS)),
        ]
        + weight_specs,
        out_specs=out_specs,
        out_shape=out_shape,
        scratch_shapes=scratch,
        compiler_params=pltpu.CompilerParams(vmem_limit_bytes=56 * MIB),
        cost_estimate=pl.CostEstimate(flops=1000, transcendentals=0, bytes_accessed=1000),
        name="step_first" if first_step else "step_own" if want_own else "step_pack",
    )(*((ids,) if want_pack else ()), helicity_start, now, *halo, prev, pot, damping, switch, *weights)


def inflow_kernel(count, want_edges, *refs):
    x_refs, refs = refs[:count], refs[count:]
    f_high, f_low, b_high, b_low, acc_ref, *refs = refs
    step = x_refs[0].shape[0] * BLK
    rows_in = count * step
    out_ref = refs[0]
    terms = refs[-1]
    product_section = lax.axis_index("sec") == 1

    @pl.when(jnp.logical_and(product_section, pl.program_id(0) == 0))
    def _():
        for k in range(HEL):
            lanes = slice(k * NA, (k + 1) * NA)
            for n, x_ref in enumerate(x_refs):
                high, low = split(x_ref[:, k].reshape(step, NA))
                terms[n * step : (n + 1) * step, lanes] = high
                terms[rows_in + n * step : rows_in + (n + 1) * step, lanes] = low

    @pl.when(product_section)
    def _():
        wide = dot(terms[...], f_high[0])
        high, low = split(wide[:rows_in] + wide[rows_in:] + dot(terms[0:rows_in], f_low[0]))
        for r in range(2):
            rows = slice(r * PTS // 2, (r + 1) * PTS // 2)
            gain = dot(b_high[rows], high) + dot(b_low[rows], high) + dot(b_high[rows], low)
            lines = slice(r * CR // 2, (r + 1) * CR // 2)
            out_ref[0, lines] = acc_ref[0, lines] + gain.reshape(CR // 2, CS, NA)

    @pl.when(jnp.logical_not(product_section))
    def _():
        out_ref[...] = acc_ref[...]

    if want_edges:
        top_ref, bottom_ref, left_ref, right_ref = refs[1:5]
        top_ref[0] = out_ref[0, 0]
        bottom_ref[0] = out_ref[0, CR - 1]
        left_ref[0] = out_ref[0, :, 0, :]
        right_ref[0] = out_ref[0, :, CS - 1, :]


def inflow_call(part, want_edges, xs, frame, blend, acc, flops=1000):
    rows_in = len(xs) * xs[0].shape[0] * BLK
    column = pl.BlockSpec((1, HEL * NA, NA), lambda n: (n, 0, 0))
    weights = pl.BlockSpec((PTS, rows_in), lambda n: (0, part))
    field = pl.BlockSpec((1, CR, CS, NA), lambda n: (n, 0, 0, 0))
    edge = pl.BlockSpec((1, CR, NA), lambda n: (n, 0, 0))
    count = 4 if want_edges else 0
    return pl.pallas_call(
        functools.partial(inflow_kernel, len(xs), want_edges),
        grid=(HEL,),
        in_specs=[whole(x.shape) for x in xs] + [column, column, weights, weights, field],
        out_specs=[field] + [edge] * count,
        out_shape=[jax.ShapeDtypeStruct((HEL, CR, CS, NA), F32)] + [jax.ShapeDtypeStruct((HEL, CR, NA), F32)] * count,
        scratch_shapes=[pltpu.VMEM((2 * rows_in, HEL * NA), BF16)],
        compiler_params=pltpu.CompilerParams(vmem_limit_bytes=56 * MIB),
        cost_estimate=pl.CostEstimate(flops=flops, transcendentals=0, bytes_accessed=1000),
        name="inflow_edges" if want_edges else "inflow",
    )(*xs, *frame, *blend, acc)


def exchange(top, bottom, left, right):
    rows, columns = lax.axis_size("rr"), lax.axis_size("sr")

    def send(piece, axis, peers, forward):
        pairs = [(i, i + 1) if forward else (i + 1, i) for i in range(peers - 1)]
        return lax.ppermute(piece, axis, pairs)

    return (
        send(bottom, "rr", rows, True),
        send(top, "rr", rows, False),
        send(right, "sr", columns, True),
        send(left, "sr", columns, False),
    )


def cross(x):
    pairs = [(s, SRCS + (s ^ (SRCS // 2))) for s in range(SRCS)]
    return lax.ppermute(x, ALL, pairs)


def spread(x):
    return lax.all_to_all(x, ("rr", "sr"), split_axis=0, concat_axis=0, tiled=True)


def per_device(
    wave_prev,
    wave_now,
    potential,
    damping,
    switch,
    angular,
    coriolis,
    helicity_start,
    frame_map,
    route_table,
    pick_slots,
    interp_weights,
):
    section = lax.axis_index("sec")
    me = lax.axis_index("rr") * lax.axis_size("sr") + lax.axis_index("sr")
    previous, current = wave_prev[0], wave_now[0]
    halo = exchange(current[:, 0], current[:, CR - 1], current[:, :, 0], current[:, :, CS - 1])
    outgoing = lax.dynamic_index_in_dim(route_table, me, axis=1, keepdims=False)
    ids = outgoing.T.reshape(2 * SRCS)

    fixed = (potential[0], damping[0], switch)

    own_1, one_1, zero_1, *rims, weights = step_call(
        True, True, True, ids, helicity_start, current, halo, previous, *fixed, angular[0], coriolis[0]
    )
    crossed_one_1 = cross(one_1)
    halo = exchange(*rims)
    relayed_1 = spread(zero_1)
    pack_shapes = [jax.ShapeDtypeStruct((SRCS, HEL, BLK, NA), F32)] * 2
    blend_shapes = [jax.ShapeDtypeStruct((PTS, PTS), BF16)] * 2
    frame_shapes = [jax.ShapeDtypeStruct((HEL, HEL * NA, NA), BF16)] * 2

    def reactant(own, halo, weights, *_):
        one, zero, *rest = step_call(
            False, False, True, ids, helicity_start, own, halo, current, *fixed, weights, others=blend_shapes + frame_shapes
        )
        return one, zero, tuple(rest[:2]), tuple(rest[2:])

    def product(own, halo, weights, picks, tiles, frame_map):
        high, low, one, zero = blend_call(picks, jnp.tile(tiles, (1, 1, 1, 128 // BLK)), pack_shapes)
        return one, zero, (high, low), frame_terms(frame_map)

    picks = pick_slots[0, 0].T.reshape(MSLOT * NBLK)
    one_2, zero_2, blend, frame = lax.cond(
        section == 0, reactant, product, own_1, halo, weights, picks, interp_weights[0, 0], frame_map
    )
    crossed_zero_1 = cross(relayed_1)
    shared = spread(jnp.where(section == 0, zero_2, crossed_one_1))
    crossed_zero_2 = cross(shared)
    one_2, shared = lax.optimization_barrier((one_2, shared))
    relayed_2 = spread(one_2)

    new_1, *rims = inflow_call(0, True, (crossed_zero_1, shared), frame, blend, own_1, 40 << 30)
    relayed_2, rims = lax.optimization_barrier((relayed_2, rims))
    first_2, last_2 = cross(relayed_2[: SRCS // 2]), cross(relayed_2[SRCS // 2 :])
    halo = exchange(*rims)
    (own_2,) = step_call(False, True, False, ids, helicity_start, new_1, halo, current, *fixed, weights)
    (new_2,) = inflow_call(0, False, (crossed_zero_2,), frame, blend, own_2)
    (new_2,) = inflow_call(3, False, (first_2,), frame, blend, new_2)
    (new_2,) = inflow_call(2, False, (last_2,), frame, blend, new_2)
    return new_1[None], new_2[None]


def solution(mesh):
    placed = (
        P("sec", None, "rr", "sr", None),
        P("sec", None, "rr", "sr", None),
        P("sec", "rr", "sr", None),
        P("sec", "rr", "sr"),
        P("rr", "sr"),
        P("sec", None, None, None),
        P("sec", None, None, None),
        P("sec"),
        P(),
        P(),
        P("rr", "sr", None, None),
        P("rr", "sr", None, None, None, None),
    )
    return jax.shard_map(
        per_device,
        mesh=mesh,
        in_specs=placed,
        out_specs=(P("sec", None, "rr", "sr", None), P("sec", None, "rr", "sr", None)),
        check_vma=False,
    )
```

```python
import functools

import jax
import jax.numpy as jnp
from jax import lax
from jax.experimental import pallas as pl
from jax.experimental.pallas import tpu as pltpu
from jax.sharding import PartitionSpec as P

JTOT = 23
HEL = 4
NA = 256
CR = 32
CS = 32
PTS = CR * CS
BLK = 8
NBLK = PTS // BLK
SRCS = 64
MSLOT = 4
TI = 8
ROWS = TI * CS
MIB = 1 << 20

kinetic = 0.08
rotor_scale = 0.1
centrifugal = 0.0005
coriolis_scale = 0.005
F32 = jnp.float32
BF16 = jnp.bfloat16
ALL = ("sec", "rr", "sr")


def dot(a, b):
    return jnp.dot(a, b, preferred_element_type=F32)


def split(x):
    high = x.astype(BF16)
    return high, (x - high.astype(F32)).astype(BF16)


def whole(shape, space=pltpu.VMEM):
    return pl.BlockSpec(shape, lambda *_: (0,) * len(shape), memory_space=space)


def smem():
    return pl.BlockSpec(memory_space=pltpu.SMEM)


def frame_terms(frame_map):
    turned = frame_map.transpose(2, 0, 1, 3).reshape(HEL, HEL * NA, NA)
    high = lax.reduce_precision(turned, 8, 7)
    return high.astype(BF16), (turned - high).astype(BF16)


def blend_kernel(pick_ref, tile_ref, high_ref, low_ref, *unused):
    lane_block = lax.broadcasted_iota(jnp.int32, (BLK, PTS), 1) // BLK

    def rows_of(b):
        total = None
        for m in range(MSLOT):
            pick = pick_ref[m * NBLK + b]
            source, slot = pick // 2, pick % 2
            column = jnp.where(slot == 0, source, SRCS + (source ^ (SRCS // 2)))
            spread_tile = jnp.concatenate([tile_ref[b, m]] * (PTS // 128), axis=1)
            piece = jnp.where(lane_block == column, spread_tile, 0.0)
            total = piece if total is None else total + piece
        return total

    def pair(n, carry):
        row = pl.multiple_of(n * 2 * BLK, 2 * BLK)
        high, low = split(jnp.concatenate([rows_of(2 * n), rows_of(2 * n + 1)], axis=0))
        high_ref[pl.ds(row, 2 * BLK), :] = high
        low_ref[pl.ds(row, 2 * BLK), :] = low
        return carry

    lax.fori_loop(0, NBLK // 2, pair, 0)


def untouched(shapes):
    return [pl.BlockSpec(memory_space=pl.ANY)] * len(shapes), list(shapes)


def blend_call(picks, tiles, others):
    specs, shapes = untouched(others)
    return pl.pallas_call(
        blend_kernel,
        in_specs=[smem(), pl.BlockSpec(memory_space=pltpu.VMEM)],
        out_specs=[pl.BlockSpec(memory_space=pltpu.VMEM)] * 2 + specs,
        out_shape=[jax.ShapeDtypeStruct((PTS, PTS), BF16)] * 2 + shapes,
        compiler_params=pltpu.CompilerParams(vmem_limit_bytes=24 * MIB),
        cost_estimate=pl.CostEstimate(flops=8 * MIB, transcendentals=0, bytes_accessed=6 * MIB),
        name="blend_matrix",
    )(picks, tiles)


ABOVE = (4, 5, 7)
BELOW = (6, 8, 9)


def step_kernel(first_step, want_own, want_pack, *refs):
    refs = list(refs)
    ids = refs.pop(0) if want_pack else None
    start_ref, now, up, down, left, right, prev, pot, damping, switch = refs[:10]
    refs = refs[10:]
    if first_step:
        angular, coriolis = refs.pop(0), refs.pop(0)
    else:
        w_ref = refs.pop(0)
    own_ref = refs.pop(0) if want_own else None
    if want_pack:
        pack_ones = [refs.pop(0) for _ in range(2 if first_step else 1)]
        pack_zero = refs.pop(0)
    if first_step:
        top_ref, bottom_ref, left_ref, right_ref, w_ref = refs[:5]
        refs = refs[5:]
    rot, mix = refs[-3:-1] if want_pack else refs[-2:]
    absorbed = refs[-1] if want_pack else None
    chunk = pl.program_id(0)
    first = chunk * TI
    lowest = start_ref[0]
    total_j = float(JTOT * (JTOT + 1))

    if first_step:

        @pl.when(chunk == 0)
        def _():
            def put(n, w):
                high, low = split(w)
                w_ref[n, 0:NA] = high
                w_ref[n, NA : 2 * NA] = high
                w_ref[n, 2 * NA : 3 * NA] = low

            for k in range(HEL):
                put(k, angular[k].T)
            for k in range(HEL - 1):
                helicity = (lowest + k).astype(F32)
                ladder = coriolis_scale * jnp.sqrt(jnp.full((NA, NA), total_j - helicity * (helicity + 1.0), F32))
                scaled = ladder * coriolis[k]
                put(ABOVE[k], scaled.T)
                put(BELOW[k], scaled)

    parts = []
    for k in range(HEL):
        high, low = split(now[k, pl.ds(first, TI)].reshape(ROWS, NA))
        parts.append(jnp.concatenate([high, low, high], axis=1))
    for k in range(HEL):
        rot[k] = dot(parts[k], w_ref[k])
    mix[0] = dot(parts[1], w_ref[ABOVE[0]])
    for k in (1, 2):
        both = jnp.concatenate([parts[k + 1], parts[k - 1]], axis=1)
        mix[k] = dot(both, w_ref[ABOVE[k] : ABOVE[k] + 2].reshape(6 * NA, NA))
    mix[3] = dot(parts[2], w_ref[BELOW[2]])

    bond = lax.broadcasted_iota(jnp.int32, (CS, NA), 0)
    diagonal = lax.broadcasted_iota(jnp.int32, (CS, CS), 0) == lax.broadcasted_iota(jnp.int32, (CS, CS), 1)
    live = jnp.where(lax.axis_index("sec") == 0, 1.0, 0.0)

    def factor(position, cells):
        base = 1.0 + 3.0 * position.astype(F32) / float(cells)
        return 1.0 / (base * base)

    bond_cells = lax.axis_size("sr") * CS
    bond_factor = factor(lax.axis_index("sr") * CS + bond, bond_cells)
    radial_cells = lax.axis_size("rr") * CR
    radial_start = lax.axis_index("rr") * CR + first
    helicities = [(lowest + k).astype(F32) for k in range(HEL)]
    centre = [centrifugal * (total_j - 2.0 * h * h) for h in helicities]

    def column(ref, i):
        line = jnp.broadcast_to(ref[pl.ds(i, 1), :], (CS, CS))
        return jnp.sum(jnp.where(diagonal, line, 0.0), axis=1, keepdims=True)

    def row(t, carry):
        i = first + t
        u = factor(jnp.full((CS, NA), radial_start + t, jnp.int32), radial_cells)
        start = pl.multiple_of(t * CS, CS)
        damp = jnp.broadcast_to(column(damping, i), (CS, NA))
        share = jnp.broadcast_to(column(switch, i) * live, (CS, NA))
        spin = rotor_scale * (u + bond_factor)
        well = pot[t] + 4.0 * kinetic
        for k in range(HEL):
            v = now[k, i]
            before = jnp.where(i == 0, up[k], now[k, jnp.maximum(i - 1, 0)])
            after = jnp.where(i == CR - 1, down[k], now[k, jnp.minimum(i + 1, CR - 1)])
            lower = jnp.where(bond == 0, left[k, pl.ds(i, 1), :], pltpu.roll(v, 1, 0))
            upper = jnp.where(bond == CS - 1, right[k, pl.ds(i, 1), :], pltpu.roll(v, CS - 1, 0))
            applied = (
                (well + u * centre[k]) * v
                - kinetic * ((before + after) + (lower + upper))
                + spin * rot[k, pl.ds(start, CS), :]
                + u * mix[k, pl.ds(start, CS), :]
            )
            renewed = damp * (2.0 * applied - damp * prev[k, t])
            taken = share * renewed
            if want_own:
                own_ref[k, t] = renewed - taken
            if want_pack:
                absorbed[k, i] = taken
        return carry

    lax.fori_loop(0, TI, row, 0)

    if first_step:
        for k in range(HEL):
            left_ref[k, pl.ds(pl.multiple_of(first, TI), TI), :] = own_ref[k, :, 0, :]
            right_ref[k, pl.ds(pl.multiple_of(first, TI), TI), :] = own_ref[k, :, CS - 1, :]

        @pl.when(chunk == 0)
        def _():
            top_ref[...] = own_ref[:, 0]

        @pl.when(chunk == CR // TI - 1)
        def _():
            bottom_ref[...] = own_ref[:, TI - 1]

    if want_pack:

        @pl.when(chunk == CR // TI - 1)
        def _():
            def copy(slot, target, to):
                e = jnp.maximum(ids[slot], 0)
                i = e // (CS // BLK)
                j = pl.multiple_of((e % (CS // BLK)) * BLK, BLK)
                for k in range(HEL):
                    target[to, k] = absorbed[k, i, pl.ds(j, BLK), :]

            def move(q, carry):
                half = SRCS // 2
                copy(q + half, pack_zero, q)
                copy(q, pack_zero, q + half)
                for n in range(2):
                    if first_step:
                        copy(SRCS + half * n + q, pack_ones[n], q)
                    else:
                        copy(SRCS + half * (1 - n) + q, pack_ones[0], half * n + q)
                return carry

            lax.fori_loop(0, SRCS // 2, move, 0)


def step_call(first_step, want_own, want_pack, ids, helicity_start, now, halo, prev, pot, damping, switch, *weights, others=()):
    field = (HEL, CR, CS, NA)
    edge = (HEL, CR, NA)
    stack = (10, 3 * NA, NA)
    rows = pl.BlockSpec((HEL, TI, CS, NA), lambda c: (0, c, 0, 0))
    out_specs, out_shape, scratch = [], [], []
    if want_own:
        out_specs.append(rows)
        out_shape.append(jax.ShapeDtypeStruct(field, F32))
    if want_pack:
        half = (SRCS // 2, HEL, BLK, NA)
        packed = (SRCS, HEL, BLK, NA)
        packs = (half, half, packed) if first_step else (packed, packed)
        out_specs += [whole(n) for n in packs]
        out_shape += [jax.ShapeDtypeStruct(n, F32) for n in packs]
    if first_step:
        out_specs += [whole(edge)] * 4 + [whole(stack)]
        out_shape += [jax.ShapeDtypeStruct(edge, F32)] * 4 + [jax.ShapeDtypeStruct(stack, BF16)]
    specs, shapes = untouched(others)
    out_specs += specs
    out_shape += shapes
    scratch += [pltpu.VMEM((HEL, ROWS, NA), F32)] * 2
    if want_pack:
        scratch.append(pltpu.VMEM(field, F32))
    weight_specs = [whole((HEL, NA, NA)), whole((HEL - 1, NA, NA))] if first_step else [whole(stack)]
    return pl.pallas_call(
        functools.partial(step_kernel, first_step, want_own, want_pack),
        grid=(CR // TI,),
        in_specs=([smem()] if want_pack else [])
        + [
            smem(),
            whole(field),
            whole(edge),
            whole(edge),
            whole(edge),
            whole(edge),
            rows,
            pl.BlockSpec((TI, CS, NA), lambda c: (c, 0, 0)),
            whole((CR, CS)),
            whole((CR, CS)),
        ]
        + weight_specs,
        out_specs=out_specs,
        out_shape=out_shape,
        scratch_shapes=scratch,
        compiler_params=pltpu.CompilerParams(vmem_limit_bytes=56 * MIB),
        cost_estimate=pl.CostEstimate(flops=1000, transcendentals=0, bytes_accessed=1000),
        name="step_first" if first_step else "step_own" if want_own else "step_pack",
    )(*((ids,) if want_pack else ()), helicity_start, now, *halo, prev, pot, damping, switch, *weights)


def inflow_kernel(count, want_edges, *refs):
    x_refs, refs = refs[:count], refs[count:]
    f_high, f_low, b_high, b_low, acc_ref, *refs = refs
    step = x_refs[0].shape[0] * BLK
    rows_in = count * step
    out_ref = refs[0]
    terms, turned = refs[-2:]
    product_section = lax.axis_index("sec") == 1

    @pl.when(jnp.logical_and(product_section, pl.program_id(0) == 0))
    def _():
        for k in range(HEL):
            lanes = slice(k * NA, (k + 1) * NA)
            for n, x_ref in enumerate(x_refs):
                high, low = split(x_ref[:, k].reshape(step, NA))
                terms[n * step : (n + 1) * step, lanes] = high
                terms[rows_in + n * step : rows_in + (n + 1) * step, lanes] = low

    @pl.when(product_section)
    def _():
        for r in range(rows_in // 256):
            top = slice(r * 256, (r + 1) * 256)
            bottom = slice(rows_in + r * 256, rows_in + (r + 1) * 256)
            framed = dot(terms[top], f_high[0]) + dot(terms[bottom], f_high[0]) + dot(terms[top], f_low[0])
            turned[top], turned[bottom] = split(framed)
        high, low = turned[0:rows_in], turned[rows_in : 2 * rows_in]
        for r in range(PTS // 256):
            rows = slice(r * 256, (r + 1) * 256)
            gain = dot(b_high[rows], high) + dot(b_low[rows], high) + dot(b_high[rows], low)
            lines = slice(r * 256 // CS, (r + 1) * 256 // CS)
            out_ref[0, lines] = acc_ref[0, lines] + gain.reshape(256 // CS, CS, NA)

    @pl.when(jnp.logical_not(product_section))
    def _():
        out_ref[...] = acc_ref[...]

    if want_edges:
        top_ref, bottom_ref, left_ref, right_ref = refs[1:5]
        top_ref[0] = out_ref[0, 0]
        bottom_ref[0] = out_ref[0, CR - 1]
        left_ref[0] = out_ref[0, :, 0, :]
        right_ref[0] = out_ref[0, :, CS - 1, :]


def inflow_call(part, want_edges, xs, frame, blend, acc, flops=1000):
    rows_in = len(xs) * xs[0].shape[0] * BLK
    column = pl.BlockSpec((1, HEL * NA, NA), lambda n: (n, 0, 0))
    weights = pl.BlockSpec((PTS, rows_in), lambda n: (0, part))
    field = pl.BlockSpec((1, CR, CS, NA), lambda n: (n, 0, 0, 0))
    edge = pl.BlockSpec((1, CR, NA), lambda n: (n, 0, 0))
    count = 4 if want_edges else 0
    return pl.pallas_call(
        functools.partial(inflow_kernel, len(xs), want_edges),
        grid=(HEL,),
        in_specs=[whole(x.shape) for x in xs] + [column, column, weights, weights, field],
        out_specs=[field] + [edge] * count,
        out_shape=[jax.ShapeDtypeStruct((HEL, CR, CS, NA), F32)] + [jax.ShapeDtypeStruct((HEL, CR, NA), F32)] * count,
        scratch_shapes=[pltpu.VMEM((2 * rows_in, HEL * NA), BF16), pltpu.VMEM((2 * rows_in, NA), BF16)],
        compiler_params=pltpu.CompilerParams(vmem_limit_bytes=56 * MIB),
        cost_estimate=pl.CostEstimate(flops=flops, transcendentals=0, bytes_accessed=1000),
        name="inflow_edges" if want_edges else "inflow",
    )(*xs, *frame, *blend, acc)


def exchange(top, bottom, left, right):
    rows, columns = lax.axis_size("rr"), lax.axis_size("sr")

    def send(piece, axis, peers, forward):
        pairs = [(i, i + 1) if forward else (i + 1, i) for i in range(peers - 1)]
        return lax.ppermute(piece, axis, pairs)

    return (
        send(bottom, "rr", rows, True),
        send(top, "rr", rows, False),
        send(right, "sr", columns, True),
        send(left, "sr", columns, False),
    )


def cross(x):
    pairs = [(s, SRCS + (s ^ (SRCS // 2))) for s in range(SRCS)]
    return lax.ppermute(x, ALL, pairs)


def spread(x):
    return lax.all_to_all(x, ("rr", "sr"), split_axis=0, concat_axis=0, tiled=True)


def per_device(
    wave_prev,
    wave_now,
    potential,
    damping,
    switch,
    angular,
    coriolis,
    helicity_start,
    frame_map,
    route_table,
    pick_slots,
    interp_weights,
):
    section = lax.axis_index("sec")
    me = lax.axis_index("rr") * lax.axis_size("sr") + lax.axis_index("sr")
    previous, current = wave_prev[0], wave_now[0]
    halo = exchange(current[:, 0], current[:, CR - 1], current[:, :, 0], current[:, :, CS - 1])
    outgoing = lax.dynamic_index_in_dim(route_table, me, axis=1, keepdims=False)
    ids = outgoing.T.reshape(2 * SRCS)

    fixed = (potential[0], damping[0], switch)

    own_1, one_1, rest_1, zero_1, *rims, weights = step_call(
        True, True, True, ids, helicity_start, current, halo, previous, *fixed, angular[0], coriolis[0]
    )
    crossed_one_1 = cross(one_1)
    halo = exchange(*rims)
    relayed_1 = spread(zero_1)
    rest_1, halo = lax.optimization_barrier((rest_1, halo))
    crossed_rest_1 = cross(rest_1)
    pack_shapes = [jax.ShapeDtypeStruct((SRCS, HEL, BLK, NA), F32)] * 2
    blend_shapes = [jax.ShapeDtypeStruct((PTS, PTS), BF16)] * 2
    frame_shapes = [jax.ShapeDtypeStruct((HEL, HEL * NA, NA), BF16)] * 2

    def reactant(own, halo, weights, *_):
        one, zero, *rest = step_call(
            False, False, True, ids, helicity_start, own, halo, current, *fixed, weights, others=blend_shapes + frame_shapes
        )
        return one, zero, tuple(rest[:2]), tuple(rest[2:])

    def product(own, halo, weights, picks, tiles, frame_map):
        high, low, one, zero = blend_call(picks, jnp.tile(tiles, (1, 1, 1, 128 // BLK)), pack_shapes)
        return one, zero, (high, low), frame_terms(frame_map)

    picks = pick_slots[0, 0].T.reshape(MSLOT * NBLK)
    one_2, zero_2, blend, frame = lax.cond(
        section == 0, reactant, product, own_1, halo, weights, picks, interp_weights[0, 0], frame_map
    )
    crossed_zero_1 = cross(relayed_1)
    arrived_1 = jnp.concatenate([crossed_one_1, crossed_rest_1])
    shared = spread(jnp.where(section == 0, zero_2, arrived_1))
    crossed_zero_2 = cross(shared)
    one_2, shared = lax.optimization_barrier((one_2, shared))
    relayed_2 = spread(one_2)

    new_1, *rims = inflow_call(0, True, (crossed_zero_1, shared), frame, blend, own_1, 40 << 30)
    relayed_2, rims = lax.optimization_barrier((relayed_2, rims))
    first_2, last_2 = cross(relayed_2[: SRCS // 2]), cross(relayed_2[SRCS // 2 :])
    halo = exchange(*rims)
    (own_2,) = step_call(False, True, False, ids, helicity_start, new_1, halo, current, *fixed, weights)
    (new_2,) = inflow_call(0, False, (crossed_zero_2,), frame, blend, own_2)
    (new_2,) = inflow_call(3, False, (first_2,), frame, blend, new_2)
    (new_2,) = inflow_call(2, False, (last_2,), frame, blend, new_2)
    return new_1[None], new_2[None]


def solution(mesh):
    placed = (
        P("sec", None, "rr", "sr", None),
        P("sec", None, "rr", "sr", None),
        P("sec", "rr", "sr", None),
        P("sec", "rr", "sr"),
        P("rr", "sr"),
        P("sec", None, None, None),
        P("sec", None, None, None),
        P("sec"),
        P(),
        P(),
        P("rr", "sr", None, None),
        P("rr", "sr", None, None, None, None),
    )
    return jax.shard_map(
        per_device,
        mesh=mesh,
        in_specs=placed,
        out_specs=(P("sec", None, "rr", "sr", None), P("sec", None, "rr", "sr", None)),
        check_vma=False,
    )
```

```python
import functools

import jax
import jax.numpy as jnp
from jax import lax
from jax.experimental import pallas as pl
from jax.experimental.pallas import tpu as pltpu
from jax.sharding import PartitionSpec as P

JTOT = 23
HEL = 4
NA = 256
CR = 32
CS = 32
PTS = CR * CS
BLK = 8
NBLK = PTS // BLK
SRCS = 64
MSLOT = 4
TI = 8
ROWS = TI * CS
MIB = 1 << 20

kinetic = 0.08
rotor_scale = 0.1
centrifugal = 0.0005
coriolis_scale = 0.005
F32 = jnp.float32
BF16 = jnp.bfloat16
ALL = ("sec", "rr", "sr")


def dot(a, b):
    return jnp.dot(a, b, preferred_element_type=F32)


def split(x):
    high = x.astype(BF16)
    return high, (x - high.astype(F32)).astype(BF16)


def whole(shape, space=pltpu.VMEM):
    return pl.BlockSpec(shape, lambda *_: (0,) * len(shape), memory_space=space)


def smem():
    return pl.BlockSpec(memory_space=pltpu.SMEM)


def frame_terms(frame_map):
    turned = frame_map.transpose(2, 0, 1, 3).reshape(HEL, HEL * NA, NA)
    high = lax.reduce_precision(turned, 8, 7)
    return high.astype(BF16), (turned - high).astype(BF16)


def blend_kernel(pick_ref, tile_ref, high_ref, low_ref, *unused):
    lane_block = lax.broadcasted_iota(jnp.int32, (BLK, PTS), 1) // BLK

    def rows_of(b):
        total = None
        for m in range(MSLOT):
            pick = pick_ref[m * NBLK + b]
            source, slot = pick // 2, pick % 2
            column = jnp.where(slot == 0, source, SRCS + (source ^ (SRCS // 2)))
            spread_tile = jnp.concatenate([tile_ref[b, m]] * (PTS // 128), axis=1)
            piece = jnp.where(lane_block == column, spread_tile, 0.0)
            total = piece if total is None else total + piece
        return total

    def pair(n, carry):
        row = pl.multiple_of(n * 2 * BLK, 2 * BLK)
        high, low = split(jnp.concatenate([rows_of(2 * n), rows_of(2 * n + 1)], axis=0))
        high_ref[pl.ds(row, 2 * BLK), :] = high
        low_ref[pl.ds(row, 2 * BLK), :] = low
        return carry

    lax.fori_loop(0, NBLK // 2, pair, 0)


def untouched(shapes):
    return [pl.BlockSpec(memory_space=pl.ANY)] * len(shapes), list(shapes)


def blend_call(picks, tiles, others):
    specs, shapes = untouched(others)
    return pl.pallas_call(
        blend_kernel,
        in_specs=[smem(), pl.BlockSpec(memory_space=pltpu.VMEM)],
        out_specs=[pl.BlockSpec(memory_space=pltpu.VMEM)] * 2 + specs,
        out_shape=[jax.ShapeDtypeStruct((PTS, PTS), BF16)] * 2 + shapes,
        compiler_params=pltpu.CompilerParams(vmem_limit_bytes=24 * MIB),
        cost_estimate=pl.CostEstimate(flops=8 * MIB, transcendentals=0, bytes_accessed=6 * MIB),
        name="blend_matrix",
    )(picks, tiles)


ABOVE = (4, 5, 7)
BELOW = (6, 8, 9)


def step_kernel(first_step, want_own, want_pack, *refs):
    refs = list(refs)
    ids = refs.pop(0) if want_pack else None
    start_ref, now, up, down, left, right, prev, pot, damping, switch = refs[:10]
    refs = refs[10:]
    if first_step:
        angular, coriolis = refs.pop(0), refs.pop(0)
    else:
        w_ref = refs.pop(0)
    own_ref = refs.pop(0) if want_own else None
    if want_pack:
        pack_one, pack_zero = refs.pop(0), refs.pop(0)
    if first_step:
        top_ref, bottom_ref, left_ref, right_ref, w_ref = refs[:5]
        refs = refs[5:]
    rot, mix = refs[-3:-1] if want_pack else refs[-2:]
    absorbed = refs[-1] if want_pack else None
    chunk = pl.program_id(0)
    first = chunk * TI
    lowest = start_ref[0]
    total_j = float(JTOT * (JTOT + 1))

    if first_step:

        @pl.when(chunk == 0)
        def _():
            def put(n, w):
                w_ref[n, 0], w_ref[n, 1] = split(w)

            for k in range(HEL):
                put(k, angular[k].T)
            for k in range(HEL - 1):
                helicity = (lowest + k).astype(F32)
                ladder = coriolis_scale * jnp.sqrt(jnp.full((NA, NA), total_j - helicity * (helicity + 1.0), F32))
                scaled = ladder * coriolis[k]
                put(ABOVE[k], scaled.T)
                put(BELOW[k], scaled)

    parts = [split(now[k, pl.ds(first, TI)].reshape(ROWS, NA)) for k in range(HEL)]

    def product(k, n):
        high, low = parts[k]
        return dot(high, w_ref[n, 0]) + dot(low, w_ref[n, 0]) + dot(high, w_ref[n, 1])

    for k in range(HEL):
        rot[k] = product(k, k)
    mix[0] = product(1, ABOVE[0])
    for k in (1, 2):
        mix[k] = product(k + 1, ABOVE[k]) + product(k - 1, BELOW[k - 1])
    mix[3] = product(2, BELOW[2])

    bond = lax.broadcasted_iota(jnp.int32, (CS, NA), 0)
    diagonal = lax.broadcasted_iota(jnp.int32, (CS, CS), 0) == lax.broadcasted_iota(jnp.int32, (CS, CS), 1)
    live = jnp.where(lax.axis_index("sec") == 0, 1.0, 0.0)

    def factor(position, cells):
        base = 1.0 + 3.0 * position.astype(F32) / float(cells)
        return 1.0 / (base * base)

    bond_cells = lax.axis_size("sr") * CS
    bond_factor = factor(lax.axis_index("sr") * CS + bond, bond_cells)
    radial_cells = lax.axis_size("rr") * CR
    radial_start = lax.axis_index("rr") * CR + first
    helicities = [(lowest + k).astype(F32) for k in range(HEL)]
    centre = [centrifugal * (total_j - 2.0 * h * h) for h in helicities]

    def column(ref, i):
        line = jnp.broadcast_to(ref[pl.ds(i, 1), :], (CS, CS))
        return jnp.sum(jnp.where(diagonal, line, 0.0), axis=1, keepdims=True)

    def row(t):
        i = first + t
        u = factor(jnp.full((CS, NA), radial_start + t, jnp.int32), radial_cells)
        start = t * CS
        damp = jnp.broadcast_to(column(damping, i), (CS, NA))
        share = jnp.broadcast_to(column(switch, i) * live, (CS, NA))
        spin = rotor_scale * (u + bond_factor)
        well = pot[t] + 4.0 * kinetic
        for k in range(HEL):
            v = now[k, i]
            before = jnp.where(i == 0, up[k], now[k, jnp.maximum(i - 1, 0)])
            after = jnp.where(i == CR - 1, down[k], now[k, jnp.minimum(i + 1, CR - 1)])
            lower = jnp.where(bond == 0, left[k, pl.ds(i, 1), :], pltpu.roll(v, 1, 0))
            upper = jnp.where(bond == CS - 1, right[k, pl.ds(i, 1), :], pltpu.roll(v, CS - 1, 0))
            applied = (
                (well + u * centre[k]) * v
                - kinetic * ((before + after) + (lower + upper))
                + spin * rot[k, start : start + CS]
                + u * mix[k, start : start + CS]
            )
            renewed = damp * (2.0 * applied - damp * prev[k, t])
            taken = share * renewed
            if want_own:
                own_ref[k, t] = renewed - taken
            if want_pack:
                absorbed[k, i] = taken

    for t in range(TI):
        row(t)

    if first_step:
        for k in range(HEL):
            left_ref[k, pl.ds(pl.multiple_of(first, TI), TI), :] = own_ref[k, :, 0, :]
            right_ref[k, pl.ds(pl.multiple_of(first, TI), TI), :] = own_ref[k, :, CS - 1, :]

        @pl.when(chunk == 0)
        def _():
            top_ref[...] = own_ref[:, 0]

        @pl.when(chunk == CR // TI - 1)
        def _():
            bottom_ref[...] = own_ref[:, TI - 1]

    if want_pack:

        @pl.when(chunk == CR // TI - 1)
        def _():
            def copy(slot, target, to):
                e = jnp.maximum(ids[slot], 0)
                i = e // (CS // BLK)
                j = pl.multiple_of((e % (CS // BLK)) * BLK, BLK)
                for k in range(HEL):
                    target[to, k] = absorbed[k, i, pl.ds(j, BLK), :]

            def move(q, carry):
                half = SRCS // 2
                copy(q + half, pack_zero, q)
                copy(q, pack_zero, q + half)
                for n in range(2):
                    copy(SRCS + half * (n if first_step else 1 - n) + q, pack_one, half * n + q)
                return carry

            lax.fori_loop(0, SRCS // 2, move, 0)


def step_call(first_step, want_own, want_pack, ids, helicity_start, now, halo, prev, pot, damping, switch, *weights, others=()):
    field = (HEL, CR, CS, NA)
    edge = (HEL, CR, NA)
    stack = (10, 2, NA, NA)
    rows = pl.BlockSpec((HEL, TI, CS, NA), lambda c: (0, c, 0, 0))
    out_specs, out_shape, scratch = [], [], []
    if want_own:
        out_specs.append(rows)
        out_shape.append(jax.ShapeDtypeStruct(field, F32))
    if want_pack:
        packed = (SRCS, HEL, BLK, NA)
        out_specs += [whole(packed)] * 2
        out_shape += [jax.ShapeDtypeStruct(packed, F32)] * 2
    if first_step:
        out_specs += [whole(edge)] * 4 + [whole(stack)]
        out_shape += [jax.ShapeDtypeStruct(edge, F32)] * 4 + [jax.ShapeDtypeStruct(stack, BF16)]
    specs, shapes = untouched(others)
    out_specs += specs
    out_shape += shapes
    scratch += [pltpu.VMEM((HEL, ROWS, NA), F32)] * 2
    if want_pack:
        scratch.append(pltpu.VMEM(field, F32))
    weight_specs = [whole((HEL, NA, NA)), whole((HEL - 1, NA, NA))] if first_step else [whole(stack)]
    return pl.pallas_call(
        functools.partial(step_kernel, first_step, want_own, want_pack),
        grid=(CR // TI,),
        in_specs=([smem()] if want_pack else [])
        + [
            smem(),
            whole(field),
            whole(edge),
            whole(edge),
            whole(edge),
            whole(edge),
            rows,
            pl.BlockSpec((TI, CS, NA), lambda c: (c, 0, 0)),
            whole((CR, CS)),
            whole((CR, CS)),
        ]
        + weight_specs,
        out_specs=out_specs,
        out_shape=out_shape,
        scratch_shapes=scratch,
        compiler_params=pltpu.CompilerParams(vmem_limit_bytes=56 * MIB),
        cost_estimate=pl.CostEstimate(flops=1000, transcendentals=0, bytes_accessed=1000),
        name="step_first" if first_step else "step_own" if want_own else "step_pack",
    )(*((ids,) if want_pack else ()), helicity_start, now, *halo, prev, pot, damping, switch, *weights)


def inflow_kernel(count, want_edges, *refs):
    x_refs, refs = refs[:count], refs[count:]
    f_high, f_low, b_high, b_low, acc_ref, *refs = refs
    step = x_refs[0].shape[0] * BLK
    rows_in = count * step
    out_ref = refs[0]
    terms, turned = refs[-2:]
    product_section = lax.axis_index("sec") == 1

    @pl.when(jnp.logical_and(product_section, pl.program_id(0) == 0))
    def _():
        for k in range(HEL):
            lanes = slice(k * NA, (k + 1) * NA)
            for n, x_ref in enumerate(x_refs):
                high, low = split(x_ref[:, k].reshape(step, NA))
                terms[n * step : (n + 1) * step, lanes] = high
                terms[rows_in + n * step : rows_in + (n + 1) * step, lanes] = low

    @pl.when(product_section)
    def _():
        for r in range(rows_in // 256):
            top = slice(r * 256, (r + 1) * 256)
            bottom = slice(rows_in + r * 256, rows_in + (r + 1) * 256)
            framed = dot(terms[top], f_high[0]) + dot(terms[bottom], f_high[0]) + dot(terms[top], f_low[0])
            turned[top], turned[bottom] = split(framed)
        high, low = turned[0:rows_in], turned[rows_in : 2 * rows_in]
        for r in range(PTS // 256):
            rows = slice(r * 256, (r + 1) * 256)
            gain = dot(b_high[rows], high) + dot(b_low[rows], high) + dot(b_high[rows], low)
            lines = slice(r * 256 // CS, (r + 1) * 256 // CS)
            out_ref[0, lines] = acc_ref[0, lines] + gain.reshape(256 // CS, CS, NA)

    @pl.when(jnp.logical_not(product_section))
    def _():
        out_ref[...] = acc_ref[...]

    if want_edges:
        top_ref, bottom_ref, left_ref, right_ref = refs[1:5]
        top_ref[0] = out_ref[0, 0]
        bottom_ref[0] = out_ref[0, CR - 1]
        left_ref[0] = out_ref[0, :, 0, :]
        right_ref[0] = out_ref[0, :, CS - 1, :]


def inflow_call(part, want_edges, xs, frame, blend, acc, flops=1000):
    rows_in = len(xs) * xs[0].shape[0] * BLK
    column = pl.BlockSpec((1, HEL * NA, NA), lambda n: (n, 0, 0))
    weights = pl.BlockSpec((PTS, rows_in), lambda n: (0, part))
    field = pl.BlockSpec((1, CR, CS, NA), lambda n: (n, 0, 0, 0))
    edge = pl.BlockSpec((1, CR, NA), lambda n: (n, 0, 0))
    count = 4 if want_edges else 0
    return pl.pallas_call(
        functools.partial(inflow_kernel, len(xs), want_edges),
        grid=(HEL,),
        in_specs=[whole(x.shape) for x in xs] + [column, column, weights, weights, field],
        out_specs=[field] + [edge] * count,
        out_shape=[jax.ShapeDtypeStruct((HEL, CR, CS, NA), F32)] + [jax.ShapeDtypeStruct((HEL, CR, NA), F32)] * count,
        scratch_shapes=[pltpu.VMEM((2 * rows_in, HEL * NA), BF16), pltpu.VMEM((2 * rows_in, NA), BF16)],
        compiler_params=pltpu.CompilerParams(vmem_limit_bytes=56 * MIB),
        cost_estimate=pl.CostEstimate(flops=flops, transcendentals=0, bytes_accessed=1000),
        name="inflow_edges" if want_edges else "inflow",
    )(*xs, *frame, *blend, acc)


def exchange(top, bottom, left, right):
    rows, columns = lax.axis_size("rr"), lax.axis_size("sr")

    def send(piece, axis, peers, forward):
        pairs = [(i, i + 1) if forward else (i + 1, i) for i in range(peers - 1)]
        return lax.ppermute(piece, axis, pairs)

    return (
        send(bottom, "rr", rows, True),
        send(top, "rr", rows, False),
        send(right, "sr", columns, True),
        send(left, "sr", columns, False),
    )


def cross(x):
    pairs = [(s, SRCS + (s ^ (SRCS // 2))) for s in range(SRCS)]
    return lax.ppermute(x, ALL, pairs)


def spread(x):
    return lax.all_to_all(x, ("rr", "sr"), split_axis=0, concat_axis=0, tiled=True)


def per_device(
    wave_prev,
    wave_now,
    potential,
    damping,
    switch,
    angular,
    coriolis,
    helicity_start,
    frame_map,
    route_table,
    pick_slots,
    interp_weights,
):
    section = lax.axis_index("sec")
    me = lax.axis_index("rr") * lax.axis_size("sr") + lax.axis_index("sr")
    previous, current = wave_prev[0], wave_now[0]
    halo = exchange(current[:, 0], current[:, CR - 1], current[:, :, 0], current[:, :, CS - 1])
    outgoing = lax.dynamic_index_in_dim(route_table, me, axis=1, keepdims=False)
    ids = outgoing.T.reshape(2 * SRCS)

    fixed = (potential[0], damping[0], switch)

    own_1, one_1, zero_1, *rims, weights = step_call(
        True, True, True, ids, helicity_start, current, halo, previous, *fixed, angular[0], coriolis[0]
    )
    crossed_one_1 = cross(one_1)
    halo = exchange(*rims)
    relayed_1 = spread(zero_1)
    pack_shapes = [jax.ShapeDtypeStruct((SRCS, HEL, BLK, NA), F32)] * 2
    blend_shapes = [jax.ShapeDtypeStruct((PTS, PTS), BF16)] * 2
    frame_shapes = [jax.ShapeDtypeStruct((HEL, HEL * NA, NA), BF16)] * 2

    def reactant(own, halo, weights, *_):
        one, zero, *rest = step_call(
            False, False, True, ids, helicity_start, own, halo, current, *fixed, weights, others=blend_shapes + frame_shapes
        )
        return one, zero, tuple(rest[:2]), tuple(rest[2:])

    def product(own, halo, weights, picks, tiles, frame_map):
        high, low, one, zero = blend_call(picks, jnp.tile(tiles, (1, 1, 1, 128 // BLK)), pack_shapes)
        return one, zero, (high, low), frame_terms(frame_map)

    picks = pick_slots[0, 0].T.reshape(MSLOT * NBLK)
    one_2, zero_2, blend, frame = lax.cond(
        section == 0, reactant, product, own_1, halo, weights, picks, interp_weights[0, 0], frame_map
    )
    crossed_zero_1 = cross(relayed_1)
    shared = spread(jnp.where(section == 0, zero_2, crossed_one_1))
    crossed_zero_2 = cross(shared)
    one_2, shared = lax.optimization_barrier((one_2, shared))
    relayed_2 = spread(one_2)

    new_1, *rims = inflow_call(0, True, (crossed_zero_1, shared), frame, blend, own_1, 40 << 30)
    relayed_2, rims = lax.optimization_barrier((relayed_2, rims))
    first_2, last_2 = cross(relayed_2[: SRCS // 2]), cross(relayed_2[SRCS // 2 :])
    halo = exchange(*rims)
    (own_2,) = step_call(False, True, False, ids, helicity_start, new_1, halo, current, *fixed, weights)
    (new_2,) = inflow_call(0, False, (crossed_zero_2,), frame, blend, own_2)
    (new_2,) = inflow_call(3, False, (first_2,), frame, blend, new_2)
    (new_2,) = inflow_call(2, False, (last_2,), frame, blend, new_2)
    return new_1[None], new_2[None]


def solution(mesh):
    placed = (
        P("sec", None, "rr", "sr", None),
        P("sec", None, "rr", "sr", None),
        P("sec", "rr", "sr", None),
        P("sec", "rr", "sr"),
        P("rr", "sr"),
        P("sec", None, None, None),
        P("sec", None, None, None),
        P("sec"),
        P(),
        P(),
        P("rr", "sr", None, None),
        P("rr", "sr", None, None, None, None),
    )
    return jax.shard_map(
        per_device,
        mesh=mesh,
        in_specs=placed,
        out_specs=(P("sec", None, "rr", "sr", None), P("sec", None, "rr", "sr", None)),
        check_vma=False,
    )
```

```python
import functools

import jax
import jax.numpy as jnp
from jax import lax
from jax.experimental import pallas as pl
from jax.experimental.pallas import tpu as pltpu
from jax.sharding import PartitionSpec as P

JTOT = 23
HEL = 4
NA = 256
CR = 32
CS = 32
PTS = CR * CS
BLK = 8
NBLK = PTS // BLK
SRCS = 64
MSLOT = 4
TI = 8
ROWS = TI * CS
MIB = 1 << 20

kinetic = 0.08
rotor_scale = 0.1
centrifugal = 0.0005
coriolis_scale = 0.005
F32 = jnp.float32
BF16 = jnp.bfloat16
ALL = ("sec", "rr", "sr")


def dot(a, b):
    return jnp.dot(a, b, preferred_element_type=F32)


def split(x):
    high = x.astype(BF16)
    return high, (x - high.astype(F32)).astype(BF16)


def whole(shape, space=pltpu.VMEM):
    return pl.BlockSpec(shape, lambda *_: (0,) * len(shape), memory_space=space)


def smem():
    return pl.BlockSpec(memory_space=pltpu.SMEM)


def frame_terms(frame_map):
    turned = frame_map.transpose(2, 0, 1, 3).reshape(HEL, HEL * NA, NA)
    high = lax.reduce_precision(turned, 8, 7)
    return high.astype(BF16), (turned - high).astype(BF16)


def blend_kernel(pick_ref, tile_ref, high_ref, low_ref, *unused):
    lane_block = lax.broadcasted_iota(jnp.int32, (BLK, PTS), 1) // BLK

    def rows_of(b):
        total = None
        for m in range(MSLOT):
            pick = pick_ref[m * NBLK + b]
            source, slot = pick // 2, pick % 2
            column = jnp.where(slot == 0, source, SRCS + (source ^ (SRCS // 2)))
            spread_tile = jnp.concatenate([tile_ref[b, m]] * (PTS // 128), axis=1)
            piece = jnp.where(lane_block == column, spread_tile, 0.0)
            total = piece if total is None else total + piece
        return total

    def pair(n, carry):
        row = pl.multiple_of(n * 2 * BLK, 2 * BLK)
        high, low = split(jnp.concatenate([rows_of(2 * n), rows_of(2 * n + 1)], axis=0))
        high_ref[pl.ds(row, 2 * BLK), :] = high
        low_ref[pl.ds(row, 2 * BLK), :] = low
        return carry

    lax.fori_loop(0, NBLK // 2, pair, 0)


def untouched(shapes):
    return [pl.BlockSpec(memory_space=pl.ANY)] * len(shapes), list(shapes)


def blend_call(picks, tiles, others):
    specs, shapes = untouched(others)
    return pl.pallas_call(
        blend_kernel,
        in_specs=[smem(), pl.BlockSpec(memory_space=pltpu.VMEM)],
        out_specs=[pl.BlockSpec(memory_space=pltpu.VMEM)] * 2 + specs,
        out_shape=[jax.ShapeDtypeStruct((PTS, PTS), BF16)] * 2 + shapes,
        compiler_params=pltpu.CompilerParams(vmem_limit_bytes=24 * MIB),
        cost_estimate=pl.CostEstimate(flops=8 * MIB, transcendentals=0, bytes_accessed=6 * MIB),
        name="blend_matrix",
    )(picks, tiles)


ABOVE = (4, 5, 7)
BELOW = (6, 8, 9)


def step_kernel(first_step, want_own, want_pack, *refs):
    refs = list(refs)
    ids = refs.pop(0) if want_pack else None
    start_ref, now, above, below, up, down, left, right, prev, pot, damping, switch = refs[:12]
    refs = refs[12:]
    if first_step:
        angular, coriolis = refs.pop(0), refs.pop(0)
    else:
        w_ref = refs.pop(0)
    own_ref = refs.pop(0) if want_own else None
    if want_pack:
        pack_one, pack_zero = refs.pop(0), refs.pop(0)
    if first_step:
        top_ref, bottom_ref, left_ref, right_ref, w_ref = refs[:5]
        refs = refs[5:]
    rot, mix = refs[-3:-1] if want_pack else refs[-2:]
    absorbed = refs[-1] if want_pack else None
    chunk = pl.program_id(0)
    first = chunk * TI
    lowest = start_ref[0]
    total_j = float(JTOT * (JTOT + 1))

    if first_step:

        @pl.when(chunk == 0)
        def _():
            def put(n, w):
                w_ref[n, 0], w_ref[n, 1] = split(w)

            for k in range(HEL):
                put(k, angular[k].T)
            for k in range(HEL - 1):
                helicity = (lowest + k).astype(F32)
                ladder = coriolis_scale * jnp.sqrt(jnp.full((NA, NA), total_j - helicity * (helicity + 1.0), F32))
                scaled = ladder * coriolis[k]
                put(ABOVE[k], scaled.T)
                put(BELOW[k], scaled)

    parts = [split(now[k].reshape(ROWS, NA)) for k in range(HEL)]

    def product(k, n):
        high, low = parts[k]
        return dot(high, w_ref[n, 0]) + dot(low, w_ref[n, 0]) + dot(high, w_ref[n, 1])

    for k in range(HEL):
        rot[k] = product(k, k)
    mix[0] = product(1, ABOVE[0])
    for k in (1, 2):
        mix[k] = product(k + 1, ABOVE[k]) + product(k - 1, BELOW[k - 1])
    mix[3] = product(2, BELOW[2])

    bond = lax.broadcasted_iota(jnp.int32, (CS, NA), 0)
    diagonal = lax.broadcasted_iota(jnp.int32, (CS, CS), 0) == lax.broadcasted_iota(jnp.int32, (CS, CS), 1)
    live = jnp.where(lax.axis_index("sec") == 0, 1.0, 0.0)

    def factor(position, cells):
        base = 1.0 + 3.0 * position.astype(F32) / float(cells)
        return 1.0 / (base * base)

    bond_cells = lax.axis_size("sr") * CS
    bond_factor = factor(lax.axis_index("sr") * CS + bond, bond_cells)
    radial_cells = lax.axis_size("rr") * CR
    radial_start = lax.axis_index("rr") * CR + first
    helicities = [(lowest + k).astype(F32) for k in range(HEL)]
    centre = [centrifugal * (total_j - 2.0 * h * h) for h in helicities]

    def column(ref, i):
        line = jnp.broadcast_to(ref[pl.ds(i, 1), :], (CS, CS))
        return jnp.sum(jnp.where(diagonal, line, 0.0), axis=1, keepdims=True)

    def row(t):
        i = first + t
        u = factor(jnp.full((CS, NA), radial_start + t, jnp.int32), radial_cells)
        start = t * CS
        damp = jnp.broadcast_to(column(damping, i), (CS, NA))
        share = jnp.broadcast_to(column(switch, i) * live, (CS, NA))
        spin = rotor_scale * (u + bond_factor)
        well = pot[t] + 4.0 * kinetic
        for k in range(HEL):
            v = now[k, t]
            before = now[k, t - 1] if t > 0 else jnp.where(chunk == 0, up[k], above[k, 0])
            after = now[k, t + 1] if t < TI - 1 else jnp.where(chunk == CR // TI - 1, down[k], below[k, 0])
            lower = jnp.where(bond == 0, left[k, pl.ds(i, 1), :], pltpu.roll(v, 1, 0))
            upper = jnp.where(bond == CS - 1, right[k, pl.ds(i, 1), :], pltpu.roll(v, CS - 1, 0))
            applied = (
                (well + u * centre[k]) * v
                - kinetic * ((before + after) + (lower + upper))
                + spin * rot[k, start : start + CS]
                + u * mix[k, start : start + CS]
            )
            renewed = damp * (2.0 * applied - damp * prev[k, t])
            taken = share * renewed
            if want_own:
                own_ref[k, t] = renewed - taken
            if want_pack:
                absorbed[k, i] = taken

    for t in range(TI):
        row(t)

    if first_step:
        for k in range(HEL):
            left_ref[k, pl.ds(pl.multiple_of(first, TI), TI), :] = own_ref[k, :, 0, :]
            right_ref[k, pl.ds(pl.multiple_of(first, TI), TI), :] = own_ref[k, :, CS - 1, :]

        @pl.when(chunk == 0)
        def _():
            top_ref[...] = own_ref[:, 0]

        @pl.when(chunk == CR // TI - 1)
        def _():
            bottom_ref[...] = own_ref[:, TI - 1]

    if want_pack:

        @pl.when(chunk == CR // TI - 1)
        def _():
            def copy(slot, target, to):
                e = jnp.maximum(ids[slot], 0)
                i = e // (CS // BLK)
                j = pl.multiple_of((e % (CS // BLK)) * BLK, BLK)
                for k in range(HEL):
                    target[to, k] = absorbed[k, i, pl.ds(j, BLK), :]

            def move(q, carry):
                half = SRCS // 2
                copy(q + half, pack_zero, q)
                copy(q, pack_zero, q + half)
                for n in range(2):
                    copy(SRCS + half * (n if first_step else 1 - n) + q, pack_one, half * n + q)
                return carry

            lax.fori_loop(0, SRCS // 2, move, 0)


def step_call(first_step, want_own, want_pack, ids, helicity_start, now, halo, prev, pot, damping, switch, *weights, others=()):
    field = (HEL, CR, CS, NA)
    edge = (HEL, CR, NA)
    stack = (10, 2, NA, NA)
    rows = pl.BlockSpec((HEL, TI, CS, NA), lambda c: (0, c, 0, 0))
    out_specs, out_shape, scratch = [], [], []
    if want_own:
        out_specs.append(rows)
        out_shape.append(jax.ShapeDtypeStruct(field, F32))
    if want_pack:
        packed = (SRCS, HEL, BLK, NA)
        out_specs += [whole(packed)] * 2
        out_shape += [jax.ShapeDtypeStruct(packed, F32)] * 2
    if first_step:
        out_specs += [whole(edge)] * 4 + [whole(stack)]
        out_shape += [jax.ShapeDtypeStruct(edge, F32)] * 4 + [jax.ShapeDtypeStruct(stack, BF16)]
    specs, shapes = untouched(others)
    out_specs += specs
    out_shape += shapes
    scratch += [pltpu.VMEM((HEL, ROWS, NA), F32)] * 2
    if want_pack:
        scratch.append(pltpu.VMEM(field, F32))
    weight_specs = [whole((HEL, NA, NA)), whole((HEL - 1, NA, NA))] if first_step else [whole(stack)]
    return pl.pallas_call(
        functools.partial(step_kernel, first_step, want_own, want_pack),
        grid=(CR // TI,),
        in_specs=([smem()] if want_pack else [])
        + [
            smem(),
            rows,
            pl.BlockSpec((HEL, 1, CS, NA), lambda c: (0, jnp.maximum(c * TI - 1, 0), 0, 0)),
            pl.BlockSpec((HEL, 1, CS, NA), lambda c: (0, jnp.minimum(c * TI + TI, CR - 1), 0, 0)),
            whole(edge),
            whole(edge),
            whole(edge),
            whole(edge),
            rows,
            pl.BlockSpec((TI, CS, NA), lambda c: (c, 0, 0)),
            whole((CR, CS)),
            whole((CR, CS)),
        ]
        + weight_specs,
        out_specs=out_specs,
        out_shape=out_shape,
        scratch_shapes=scratch,
        compiler_params=pltpu.CompilerParams(vmem_limit_bytes=56 * MIB),
        cost_estimate=pl.CostEstimate(flops=1000, transcendentals=0, bytes_accessed=1000),
        name="step_first" if first_step else "step_own" if want_own else "step_pack",
    )(*((ids,) if want_pack else ()), helicity_start, now, now, now, *halo, prev, pot, damping, switch, *weights)


def inflow_kernel(count, want_edges, *refs):
    x_refs, refs = refs[:count], refs[count:]
    f_high, f_low, b_high, b_low, acc_ref, *refs = refs
    step = x_refs[0].shape[0] * BLK
    rows_in = count * step
    out_ref = refs[0]
    terms, turned = refs[-2:]
    product_section = lax.axis_index("sec") == 1

    @pl.when(jnp.logical_and(product_section, pl.program_id(0) == 0))
    def _():
        for k in range(HEL):
            lanes = slice(k * NA, (k + 1) * NA)
            for n, x_ref in enumerate(x_refs):
                high, low = split(x_ref[:, k].reshape(step, NA))
                terms[n * step : (n + 1) * step, lanes] = high
                terms[rows_in + n * step : rows_in + (n + 1) * step, lanes] = low

    @pl.when(product_section)
    def _():
        for r in range(rows_in // 256):
            top = slice(r * 256, (r + 1) * 256)
            bottom = slice(rows_in + r * 256, rows_in + (r + 1) * 256)
            framed = dot(terms[top], f_high[0]) + dot(terms[bottom], f_high[0]) + dot(terms[top], f_low[0])
            turned[top], turned[bottom] = split(framed)
        high, low = turned[0:rows_in], turned[rows_in : 2 * rows_in]
        for r in range(PTS // 256):
            rows = slice(r * 256, (r + 1) * 256)
            gain = dot(b_high[rows], high) + dot(b_low[rows], high) + dot(b_high[rows], low)
            lines = slice(r * 256 // CS, (r + 1) * 256 // CS)
            out_ref[0, lines] = acc_ref[0, lines] + gain.reshape(256 // CS, CS, NA)

    @pl.when(jnp.logical_not(product_section))
    def _():
        out_ref[...] = acc_ref[...]

    if want_edges:
        top_ref, bottom_ref, left_ref, right_ref = refs[1:5]
        top_ref[0] = out_ref[0, 0]
        bottom_ref[0] = out_ref[0, CR - 1]
        left_ref[0] = out_ref[0, :, 0, :]
        right_ref[0] = out_ref[0, :, CS - 1, :]


def inflow_call(part, want_edges, xs, frame, blend, acc, flops=1000):
    rows_in = len(xs) * xs[0].shape[0] * BLK
    column = pl.BlockSpec((1, HEL * NA, NA), lambda n: (n, 0, 0))
    weights = pl.BlockSpec((PTS, rows_in), lambda n: (0, part))
    field = pl.BlockSpec((1, CR, CS, NA), lambda n: (n, 0, 0, 0))
    edge = pl.BlockSpec((1, CR, NA), lambda n: (n, 0, 0))
    count = 4 if want_edges else 0
    return pl.pallas_call(
        functools.partial(inflow_kernel, len(xs), want_edges),
        grid=(HEL,),
        in_specs=[whole(x.shape) for x in xs] + [column, column, weights, weights, field],
        out_specs=[field] + [edge] * count,
        out_shape=[jax.ShapeDtypeStruct((HEL, CR, CS, NA), F32)] + [jax.ShapeDtypeStruct((HEL, CR, NA), F32)] * count,
        scratch_shapes=[pltpu.VMEM((2 * rows_in, HEL * NA), BF16), pltpu.VMEM((2 * rows_in, NA), BF16)],
        compiler_params=pltpu.CompilerParams(vmem_limit_bytes=56 * MIB),
        cost_estimate=pl.CostEstimate(flops=flops, transcendentals=0, bytes_accessed=1000),
        name="inflow_edges" if want_edges else "inflow",
    )(*xs, *frame, *blend, acc)


def exchange(top, bottom, left, right):
    rows, columns = lax.axis_size("rr"), lax.axis_size("sr")

    def send(piece, axis, peers, forward):
        pairs = [(i, i + 1) if forward else (i + 1, i) for i in range(peers - 1)]
        return lax.ppermute(piece, axis, pairs)

    return (
        send(bottom, "rr", rows, True),
        send(top, "rr", rows, False),
        send(right, "sr", columns, True),
        send(left, "sr", columns, False),
    )


def cross(x):
    pairs = [(s, SRCS + (s ^ (SRCS // 2))) for s in range(SRCS)]
    return lax.ppermute(x, ALL, pairs)


def spread(x):
    return lax.all_to_all(x, ("rr", "sr"), split_axis=0, concat_axis=0, tiled=True)


def per_device(
    wave_prev,
    wave_now,
    potential,
    damping,
    switch,
    angular,
    coriolis,
    helicity_start,
    frame_map,
    route_table,
    pick_slots,
    interp_weights,
):
    section = lax.axis_index("sec")
    me = lax.axis_index("rr") * lax.axis_size("sr") + lax.axis_index("sr")
    previous, current = wave_prev[0], wave_now[0]
    halo = exchange(current[:, 0], current[:, CR - 1], current[:, :, 0], current[:, :, CS - 1])
    outgoing = lax.dynamic_index_in_dim(route_table, me, axis=1, keepdims=False)
    ids = outgoing.T.reshape(2 * SRCS)

    fixed = (potential[0], damping[0], switch)

    own_1, one_1, zero_1, *rims, weights = step_call(
        True, True, True, ids, helicity_start, current, halo, previous, *fixed, angular[0], coriolis[0]
    )
    crossed_one_1 = cross(one_1)
    halo = exchange(*rims)
    relayed_1 = spread(zero_1)
    pack_shapes = [jax.ShapeDtypeStruct((SRCS, HEL, BLK, NA), F32)] * 2
    blend_shapes = [jax.ShapeDtypeStruct((PTS, PTS), BF16)] * 2
    frame_shapes = [jax.ShapeDtypeStruct((HEL, HEL * NA, NA), BF16)] * 2

    def reactant(own, halo, weights, *_):
        one, zero, *rest = step_call(
            False, False, True, ids, helicity_start, own, halo, current, *fixed, weights, others=blend_shapes + frame_shapes
        )
        return one, zero, tuple(rest[:2]), tuple(rest[2:])

    def product(own, halo, weights, picks, tiles, frame_map):
        high, low, one, zero = blend_call(picks, jnp.tile(tiles, (1, 1, 1, 128 // BLK)), pack_shapes)
        return one, zero, (high, low), frame_terms(frame_map)

    picks = pick_slots[0, 0].T.reshape(MSLOT * NBLK)
    one_2, zero_2, blend, frame = lax.cond(
        section == 0, reactant, product, own_1, halo, weights, picks, interp_weights[0, 0], frame_map
    )
    crossed_zero_1 = cross(relayed_1)
    shared = spread(jnp.where(section == 0, zero_2, crossed_one_1))
    crossed_zero_2 = cross(shared)
    one_2, shared = lax.optimization_barrier((one_2, shared))
    relayed_2 = spread(one_2)

    new_1, *rims = inflow_call(0, True, (crossed_zero_1, shared), frame, blend, own_1, 40 << 30)
    relayed_2, rims = lax.optimization_barrier((relayed_2, rims))
    first_2, last_2 = cross(relayed_2[: SRCS // 2]), cross(relayed_2[SRCS // 2 :])
    halo = exchange(*rims)
    (own_2,) = step_call(False, True, False, ids, helicity_start, new_1, halo, current, *fixed, weights)
    (new_2,) = inflow_call(0, False, (crossed_zero_2,), frame, blend, own_2)
    (new_2,) = inflow_call(3, False, (first_2,), frame, blend, new_2)
    (new_2,) = inflow_call(2, False, (last_2,), frame, blend, new_2)
    return new_1[None], new_2[None]


def solution(mesh):
    placed = (
        P("sec", None, "rr", "sr", None),
        P("sec", None, "rr", "sr", None),
        P("sec", "rr", "sr", None),
        P("sec", "rr", "sr"),
        P("rr", "sr"),
        P("sec", None, None, None),
        P("sec", None, None, None),
        P("sec"),
        P(),
        P(),
        P("rr", "sr", None, None),
        P("rr", "sr", None, None, None, None),
    )
    return jax.shard_map(
        per_device,
        mesh=mesh,
        in_specs=placed,
        out_specs=(P("sec", None, "rr", "sr", None), P("sec", None, "rr", "sr", None)),
        check_vma=False,
    )
```

```python
import functools

import jax
import jax.numpy as jnp
from jax import lax
from jax.experimental import pallas as pl
from jax.experimental.pallas import tpu as pltpu
from jax.sharding import PartitionSpec as P

JTOT = 23
HEL = 4
NA = 256
CR = 32
CS = 32
PTS = CR * CS
BLK = 8
NBLK = PTS // BLK
SRCS = 64
MSLOT = 4
TI = 8
ROWS = TI * CS
MIB = 1 << 20

kinetic = 0.08
rotor_scale = 0.1
centrifugal = 0.0005
coriolis_scale = 0.005
F32 = jnp.float32
BF16 = jnp.bfloat16
ALL = ("sec", "rr", "sr")


def dot(a, b):
    return jnp.dot(a, b, preferred_element_type=F32)


def split(x):
    high = x.astype(BF16)
    return high, (x - high.astype(F32)).astype(BF16)


def whole(shape, space=pltpu.VMEM):
    return pl.BlockSpec(shape, lambda *_: (0,) * len(shape), memory_space=space)


def smem():
    return pl.BlockSpec(memory_space=pltpu.SMEM)


def frame_terms(frame_map):
    turned = frame_map.transpose(2, 0, 1, 3).reshape(HEL, HEL * NA, NA)
    high = lax.reduce_precision(turned, 8, 7)
    return high.astype(BF16), (turned - high).astype(BF16)


def blend_kernel(pick_ref, tile_ref, high_ref, low_ref, *unused):
    lane_block = lax.broadcasted_iota(jnp.int32, (BLK, PTS), 1) // BLK

    def rows_of(b):
        total = None
        for m in range(MSLOT):
            pick = pick_ref[m * NBLK + b]
            source, slot = pick // 2, pick % 2
            column = jnp.where(slot == 0, source, SRCS + (source ^ (SRCS // 2)))
            spread_tile = jnp.concatenate([tile_ref[b, m]] * (PTS // 128), axis=1)
            piece = jnp.where(lane_block == column, spread_tile, 0.0)
            total = piece if total is None else total + piece
        return total

    def pair(n, carry):
        row = pl.multiple_of(n * 2 * BLK, 2 * BLK)
        high, low = split(jnp.concatenate([rows_of(2 * n), rows_of(2 * n + 1)], axis=0))
        high_ref[pl.ds(row, 2 * BLK), :] = high
        low_ref[pl.ds(row, 2 * BLK), :] = low
        return carry

    lax.fori_loop(0, NBLK // 2, pair, 0)


def untouched(shapes):
    return [pl.BlockSpec(memory_space=pl.ANY)] * len(shapes), list(shapes)


def blend_call(picks, tiles, others):
    specs, shapes = untouched(others)
    return pl.pallas_call(
        blend_kernel,
        in_specs=[smem(), pl.BlockSpec(memory_space=pltpu.VMEM)],
        out_specs=[pl.BlockSpec(memory_space=pltpu.VMEM)] * 2 + specs,
        out_shape=[jax.ShapeDtypeStruct((PTS, PTS), BF16)] * 2 + shapes,
        compiler_params=pltpu.CompilerParams(vmem_limit_bytes=24 * MIB),
        cost_estimate=pl.CostEstimate(flops=8 * MIB, transcendentals=0, bytes_accessed=6 * MIB),
        name="blend_matrix",
    )(picks, tiles)


ABOVE = (4, 5, 7)
BELOW = (6, 8, 9)


def step_kernel(first_step, want_own, want_pack, *refs):
    refs = list(refs)
    ids = refs.pop(0) if want_pack else None
    start_ref, now, above, below, up, down, left, right, prev, pot, damping, switch = refs[:12]
    refs = refs[12:]
    if first_step:
        angular, coriolis = refs.pop(0), refs.pop(0)
    else:
        w_ref = refs.pop(0)
    own_ref = refs.pop(0) if want_own else None
    if want_pack:
        pack_one, pack_zero = refs.pop(0), refs.pop(0)
    if first_step:
        top_ref, bottom_ref, left_ref, right_ref, w_ref = refs[:5]
        refs = refs[5:]
    rot, mix = refs[-3:-1] if want_pack else refs[-2:]
    absorbed = refs[-1] if want_pack else None
    chunk = pl.program_id(0)
    first = chunk * TI
    lowest = start_ref[0]
    total_j = float(JTOT * (JTOT + 1))

    if first_step:

        @pl.when(chunk == 0)
        def _():
            def put(n, w):
                w_ref[n, 0], w_ref[n, 1] = split(w)

            for k in range(HEL):
                put(k, angular[k].T)
            for k in range(HEL - 1):
                helicity = (lowest + k).astype(F32)
                ladder = coriolis_scale * jnp.sqrt(jnp.full((NA, NA), total_j - helicity * (helicity + 1.0), F32))
                scaled = ladder * coriolis[k]
                put(ABOVE[k], scaled.T)
                put(BELOW[k], scaled)

    parts = [split(now[k].reshape(ROWS, NA)) for k in range(HEL)]

    def product(k, n):
        high, low = parts[k]
        return dot(high, w_ref[n, 0]) + dot(low, w_ref[n, 0]) + dot(high, w_ref[n, 1])

    for k in range(HEL):
        rot[k] = product(k, k)
    mix[0] = product(1, ABOVE[0])
    for k in (1, 2):
        mix[k] = product(k + 1, ABOVE[k]) + product(k - 1, BELOW[k - 1])
    mix[3] = product(2, BELOW[2])

    bond = lax.broadcasted_iota(jnp.int32, (CS, NA), 0)
    diagonal = lax.broadcasted_iota(jnp.int32, (CS, CS), 0) == lax.broadcasted_iota(jnp.int32, (CS, CS), 1)
    live = jnp.where(lax.axis_index("sec") == 0, 1.0, 0.0)

    def factor(position, cells):
        base = 1.0 + 3.0 * position.astype(F32) / float(cells)
        return 1.0 / (base * base)

    bond_cells = lax.axis_size("sr") * CS
    bond_factor = factor(lax.axis_index("sr") * CS + bond, bond_cells)
    radial_cells = lax.axis_size("rr") * CR
    radial_start = lax.axis_index("rr") * CR + first
    helicities = [(lowest + k).astype(F32) for k in range(HEL)]
    centre = [centrifugal * (total_j - 2.0 * h * h) for h in helicities]

    def column(ref, i):
        line = jnp.broadcast_to(ref[pl.ds(i, 1), :], (CS, CS))
        return jnp.sum(jnp.where(diagonal, line, 0.0), axis=1, keepdims=True)

    def row(t):
        i = first + t
        u = factor(jnp.full((CS, NA), radial_start + t, jnp.int32), radial_cells)
        start = t * CS
        damp = jnp.broadcast_to(column(damping, i), (CS, NA))
        share = jnp.broadcast_to(column(switch, i) * live, (CS, NA))
        spin = rotor_scale * (u + bond_factor)
        well = pot[t] + 4.0 * kinetic
        for k in range(HEL):
            v = now[k, t]
            before = now[k, t - 1] if t > 0 else jnp.where(chunk == 0, up[k], above[k, 0])
            after = now[k, t + 1] if t < TI - 1 else jnp.where(chunk == CR // TI - 1, down[k], below[k, 0])
            lower = jnp.where(bond == 0, left[k, pl.ds(i, 1), :], pltpu.roll(v, 1, 0))
            upper = jnp.where(bond == CS - 1, right[k, pl.ds(i, 1), :], pltpu.roll(v, CS - 1, 0))
            applied = (
                (well + u * centre[k]) * v
                - kinetic * ((before + after) + (lower + upper))
                + spin * rot[k, start : start + CS]
                + u * mix[k, start : start + CS]
            )
            renewed = damp * (2.0 * applied - damp * prev[k, t])
            taken = share * renewed
            if want_own:
                own_ref[k, t] = renewed - taken
            if want_pack:
                absorbed[k, i] = taken

    for t in range(TI):
        row(t)

    if first_step:
        for k in range(HEL):
            left_ref[k, pl.ds(pl.multiple_of(first, TI), TI), :] = own_ref[k, :, 0, :]
            right_ref[k, pl.ds(pl.multiple_of(first, TI), TI), :] = own_ref[k, :, CS - 1, :]

        @pl.when(chunk == 0)
        def _():
            top_ref[...] = own_ref[:, 0]

        @pl.when(chunk == CR // TI - 1)
        def _():
            bottom_ref[...] = own_ref[:, TI - 1]

    if want_pack:

        @pl.when(chunk == CR // TI - 1)
        def _():
            def copy(slot, target, to):
                e = jnp.maximum(ids[slot], 0)
                i = e // (CS // BLK)
                j = pl.multiple_of((e % (CS // BLK)) * BLK, BLK)
                for k in range(HEL):
                    target[to, k] = absorbed[k, i, pl.ds(j, BLK), :]

            def move(q, carry):
                half = SRCS // 2
                copy(q + half, pack_zero, q)
                copy(q, pack_zero, q + half)
                for n in range(2):
                    copy(SRCS + half * (n if first_step else 1 - n) + q, pack_one, half * n + q)
                return carry

            lax.fori_loop(0, SRCS // 2, move, 0)


def step_call(first_step, want_own, want_pack, ids, helicity_start, now, halo, prev, pot, damping, switch, *weights, others=()):
    field = (HEL, CR, CS, NA)
    edge = (HEL, CR, NA)
    stack = (10, 2, NA, NA)
    rows = pl.BlockSpec((HEL, TI, CS, NA), lambda c: (0, c, 0, 0))
    out_specs, out_shape, scratch = [], [], []
    if want_own:
        out_specs.append(rows)
        out_shape.append(jax.ShapeDtypeStruct(field, F32))
    if want_pack:
        packed = (SRCS, HEL, BLK, NA)
        out_specs += [whole(packed)] * 2
        out_shape += [jax.ShapeDtypeStruct(packed, F32)] * 2
    if first_step:
        out_specs += [whole(edge)] * 4 + [whole(stack)]
        out_shape += [jax.ShapeDtypeStruct(edge, F32)] * 4 + [jax.ShapeDtypeStruct(stack, BF16)]
    specs, shapes = untouched(others)
    out_specs += specs
    out_shape += shapes
    scratch += [pltpu.VMEM((HEL, ROWS, NA), F32)] * 2
    if want_pack:
        scratch.append(pltpu.VMEM(field, F32))
    weight_specs = [whole((HEL, NA, NA)), whole((HEL - 1, NA, NA))] if first_step else [whole(stack)]
    return pl.pallas_call(
        functools.partial(step_kernel, first_step, want_own, want_pack),
        grid=(CR // TI,),
        in_specs=([smem()] if want_pack else [])
        + [
            smem(),
            rows,
            pl.BlockSpec((HEL, 1, CS, NA), lambda c: (0, jnp.maximum(c * TI - 1, 0), 0, 0)),
            pl.BlockSpec((HEL, 1, CS, NA), lambda c: (0, jnp.minimum(c * TI + TI, CR - 1), 0, 0)),
            whole(edge),
            whole(edge),
            whole(edge),
            whole(edge),
            rows,
            pl.BlockSpec((TI, CS, NA), lambda c: (c, 0, 0)),
            whole((CR, CS)),
            whole((CR, CS)),
        ]
        + weight_specs,
        out_specs=out_specs,
        out_shape=out_shape,
        scratch_shapes=scratch,
        compiler_params=pltpu.CompilerParams(vmem_limit_bytes=56 * MIB),
        cost_estimate=pl.CostEstimate(flops=1000, transcendentals=0, bytes_accessed=1000),
        name="step_first" if first_step else "step_own" if want_own else "step_pack",
    )(*((ids,) if want_pack else ()), helicity_start, now, now, now, *halo, prev, pot, damping, switch, *weights)


def inflow_kernel(count, want_edges, *refs):
    x_refs, refs = refs[:count], refs[count:]
    f_high, f_low, b_high, b_low, acc_ref, *refs = refs
    step = x_refs[0].shape[0] * BLK
    rows_in = count * step
    out_ref = refs[0]
    terms, turned = refs[-2:]
    product_section = lax.axis_index("sec") == 1

    @pl.when(jnp.logical_and(product_section, pl.program_id(0) == 0))
    def _():
        for k in range(HEL):
            lanes = slice(k * NA, (k + 1) * NA)
            for n, x_ref in enumerate(x_refs):
                high, low = split(x_ref[:, k].reshape(step, NA))
                terms[n * step : (n + 1) * step, lanes] = high
                terms[rows_in + n * step : rows_in + (n + 1) * step, lanes] = low

    @pl.when(product_section)
    def _():
        for r in range(rows_in // 256):
            top = slice(r * 256, (r + 1) * 256)
            bottom = slice(rows_in + r * 256, rows_in + (r + 1) * 256)
            framed = dot(terms[top], f_high[0]) + dot(terms[bottom], f_high[0]) + dot(terms[top], f_low[0])
            turned[top], turned[bottom] = split(framed)
        high, low = turned[0:rows_in], turned[rows_in : 2 * rows_in]
        for r in range(PTS // 256):
            rows = slice(r * 256, (r + 1) * 256)
            gain = dot(b_high[rows], high) + dot(b_low[rows], high) + dot(b_high[rows], low)
            lines = slice(r * 256 // CS, (r + 1) * 256 // CS)
            out_ref[0, lines] = acc_ref[0, lines] + gain.reshape(256 // CS, CS, NA)

    @pl.when(jnp.logical_not(product_section))
    def _():
        out_ref[...] = acc_ref[...]

    if want_edges:
        top_ref, bottom_ref, left_ref, right_ref = refs[1:5]
        top_ref[0] = out_ref[0, 0]
        bottom_ref[0] = out_ref[0, CR - 1]
        left_ref[0] = out_ref[0, :, 0, :]
        right_ref[0] = out_ref[0, :, CS - 1, :]


def inflow_call(part, want_edges, xs, frame, blend, acc, flops=1000):
    rows_in = len(xs) * xs[0].shape[0] * BLK
    column = pl.BlockSpec((1, HEL * NA, NA), lambda n: (n, 0, 0))
    weights = pl.BlockSpec((PTS, rows_in), lambda n: (0, part))
    field = pl.BlockSpec((1, CR, CS, NA), lambda n: (n, 0, 0, 0))
    edge = pl.BlockSpec((1, CR, NA), lambda n: (n, 0, 0))
    count = 4 if want_edges else 0
    return pl.pallas_call(
        functools.partial(inflow_kernel, len(xs), want_edges),
        grid=(HEL,),
        in_specs=[whole(x.shape) for x in xs] + [column, column, weights, weights, field],
        out_specs=[field] + [edge] * count,
        out_shape=[jax.ShapeDtypeStruct((HEL, CR, CS, NA), F32)] + [jax.ShapeDtypeStruct((HEL, CR, NA), F32)] * count,
        scratch_shapes=[pltpu.VMEM((2 * rows_in, HEL * NA), BF16), pltpu.VMEM((2 * rows_in, NA), BF16)],
        compiler_params=pltpu.CompilerParams(vmem_limit_bytes=56 * MIB),
        cost_estimate=pl.CostEstimate(flops=flops, transcendentals=0, bytes_accessed=1000),
        name="inflow_edges" if want_edges else "inflow",
    )(*xs, *frame, *blend, acc)


def exchange(top, bottom, left, right):
    rows, columns = lax.axis_size("rr"), lax.axis_size("sr")

    def send(piece, axis, peers, forward):
        pairs = [(i, i + 1) if forward else (i + 1, i) for i in range(peers - 1)]
        return lax.ppermute(piece, axis, pairs)

    return (
        send(bottom, "rr", rows, True),
        send(top, "rr", rows, False),
        send(right, "sr", columns, True),
        send(left, "sr", columns, False),
    )


def cross(x):
    pairs = [(s, SRCS + (s ^ (SRCS // 2))) for s in range(SRCS)]
    return lax.ppermute(x, ALL, pairs)


def spread(x):
    return lax.all_to_all(x, ("rr", "sr"), split_axis=0, concat_axis=0, tiled=True)


def per_device(
    wave_prev,
    wave_now,
    potential,
    damping,
    switch,
    angular,
    coriolis,
    helicity_start,
    frame_map,
    route_table,
    pick_slots,
    interp_weights,
):
    section = lax.axis_index("sec")
    me = lax.axis_index("rr") * lax.axis_size("sr") + lax.axis_index("sr")
    previous, current = wave_prev[0], wave_now[0]
    halo = exchange(current[:, 0], current[:, CR - 1], current[:, :, 0], current[:, :, CS - 1])
    outgoing = lax.dynamic_index_in_dim(route_table, me, axis=1, keepdims=False)
    ids = outgoing.T.reshape(2 * SRCS)

    fixed = (potential[0], damping[0], switch)

    own_1, one_1, zero_1, *rims, weights = step_call(
        True, True, True, ids, helicity_start, current, halo, previous, *fixed, angular[0], coriolis[0]
    )
    crossed_one_1 = cross(one_1)
    halo = exchange(*rims)
    relayed_1 = spread(zero_1)
    pack_shapes = [jax.ShapeDtypeStruct((SRCS, HEL, BLK, NA), F32)] * 2
    blend_shapes = [jax.ShapeDtypeStruct((PTS, PTS), BF16)] * 2

    def reactant(own, halo, weights, *_):
        one, zero, *rest = step_call(
            False, False, True, ids, helicity_start, own, halo, current, *fixed, weights, others=blend_shapes
        )
        return one, zero, tuple(rest)

    def product(own, halo, weights, picks, tiles):
        high, low, one, zero = blend_call(picks, tiles, pack_shapes)
        return one, zero, (high, low)

    late_map, late_weights, own_1 = lax.optimization_barrier((frame_map, interp_weights[0, 0], own_1))
    frame, tiles = frame_terms(late_map), jnp.tile(late_weights, (1, 1, 1, 128 // BLK))
    own_1, frame, tiles = lax.optimization_barrier((own_1, frame, tiles))
    picks = pick_slots[0, 0].T.reshape(MSLOT * NBLK)
    one_2, zero_2, blend = lax.cond(section == 0, reactant, product, own_1, halo, weights, picks, tiles)
    crossed_zero_1 = cross(relayed_1)
    shared = spread(jnp.where(section == 0, zero_2, crossed_one_1))
    crossed_zero_2 = cross(shared)
    one_2, shared = lax.optimization_barrier((one_2, shared))
    relayed_2 = spread(one_2)

    new_1, *rims = inflow_call(0, True, (crossed_zero_1, shared), frame, blend, own_1, 40 << 30)
    relayed_2, rims = lax.optimization_barrier((relayed_2, rims))
    first_2, last_2 = cross(relayed_2[: SRCS // 2]), cross(relayed_2[SRCS // 2 :])
    halo = exchange(*rims)
    (own_2,) = step_call(False, True, False, ids, helicity_start, new_1, halo, current, *fixed, weights)
    (new_2,) = inflow_call(0, False, (crossed_zero_2,), frame, blend, own_2)
    (new_2,) = inflow_call(3, False, (first_2,), frame, blend, new_2)
    (new_2,) = inflow_call(2, False, (last_2,), frame, blend, new_2)
    return new_1[None], new_2[None]


def solution(mesh):
    placed = (
        P("sec", None, "rr", "sr", None),
        P("sec", None, "rr", "sr", None),
        P("sec", "rr", "sr", None),
        P("sec", "rr", "sr"),
        P("rr", "sr"),
        P("sec", None, None, None),
        P("sec", None, None, None),
        P("sec"),
        P(),
        P(),
        P("rr", "sr", None, None),
        P("rr", "sr", None, None, None, None),
    )
    return jax.shard_map(
        per_device,
        mesh=mesh,
        in_specs=placed,
        out_specs=(P("sec", None, "rr", "sr", None), P("sec", None, "rr", "sr", None)),
        check_vma=False,
    )
```

```python
import functools

import jax
import jax.numpy as jnp
from jax import lax
from jax.experimental import pallas as pl
from jax.experimental.pallas import tpu as pltpu
from jax.sharding import PartitionSpec as P

JTOT = 23
HEL = 4
NA = 256
CR = 32
CS = 32
PTS = CR * CS
BLK = 8
NBLK = PTS // BLK
SRCS = 64
MSLOT = 4
TI = 8
ROWS = TI * CS
MIB = 1 << 20

kinetic = 0.08
rotor_scale = 0.1
centrifugal = 0.0005
coriolis_scale = 0.005
F32 = jnp.float32
BF16 = jnp.bfloat16
ALL = ("sec", "rr", "sr")


def dot(a, b):
    return jnp.dot(a, b, preferred_element_type=F32)


def split(x):
    high = x.astype(BF16)
    return high, (x - high.astype(F32)).astype(BF16)


def whole(shape, space=pltpu.VMEM):
    return pl.BlockSpec(shape, lambda *_: (0,) * len(shape), memory_space=space)


def smem():
    return pl.BlockSpec(memory_space=pltpu.SMEM)


def frame_terms(frame_map):
    turned = frame_map.transpose(2, 0, 1, 3).reshape(HEL, HEL * NA, NA)
    high = lax.reduce_precision(turned, 8, 7)
    return high.astype(BF16), (turned - high).astype(BF16)


def blend_kernel(pick_ref, tile_ref, high_ref, low_ref, *unused):
    lane_block = lax.broadcasted_iota(jnp.int32, (BLK, PTS), 1) // BLK

    def rows_of(b):
        total = None
        for m in range(MSLOT):
            pick = pick_ref[m * NBLK + b]
            source, slot = pick // 2, pick % 2
            column = jnp.where(slot == 0, source, SRCS + (source ^ (SRCS // 2)))
            spread_tile = jnp.concatenate([tile_ref[b, m]] * (PTS // 128), axis=1)
            piece = jnp.where(lane_block == column, spread_tile, 0.0)
            total = piece if total is None else total + piece
        return total

    def pair(n, carry):
        row = pl.multiple_of(n * 2 * BLK, 2 * BLK)
        high, low = split(jnp.concatenate([rows_of(2 * n), rows_of(2 * n + 1)], axis=0))
        high_ref[pl.ds(row, 2 * BLK), :] = high
        low_ref[pl.ds(row, 2 * BLK), :] = low
        return carry

    lax.fori_loop(0, NBLK // 2, pair, 0)


def untouched(shapes):
    return [pl.BlockSpec(memory_space=pl.ANY)] * len(shapes), list(shapes)


def blend_call(picks, tiles, others):
    specs, shapes = untouched(others)
    return pl.pallas_call(
        blend_kernel,
        in_specs=[smem(), pl.BlockSpec(memory_space=pltpu.VMEM)],
        out_specs=[pl.BlockSpec(memory_space=pltpu.VMEM)] * 2 + specs,
        out_shape=[jax.ShapeDtypeStruct((PTS, PTS), BF16)] * 2 + shapes,
        compiler_params=pltpu.CompilerParams(vmem_limit_bytes=24 * MIB),
        cost_estimate=pl.CostEstimate(flops=8 * MIB, transcendentals=0, bytes_accessed=6 * MIB),
        name="blend_matrix",
    )(picks, tiles)


ABOVE = (4, 5, 7)
BELOW = (6, 8, 9)


def step_kernel(first_step, want_own, want_pack, *refs):
    refs = list(refs)
    ids = refs.pop(0) if want_pack else None
    start_ref, now, above, below, up, down, left, right, prev, pot, damping, switch = refs[:12]
    refs = refs[12:]
    if first_step:
        angular, coriolis = refs.pop(0), refs.pop(0)
    else:
        w_ref = refs.pop(0)
    own_ref = refs.pop(0) if want_own else None
    if want_pack:
        pack_one, pack_zero = refs.pop(0), refs.pop(0)
    if first_step:
        top_ref, bottom_ref, left_ref, right_ref, w_ref = refs[:5]
        refs = refs[5:]
    rot, mix = refs[-3:-1] if want_pack else refs[-2:]
    absorbed = refs[-1] if want_pack else None
    chunk = pl.program_id(0)
    first = chunk * TI
    lowest = start_ref[0]
    total_j = float(JTOT * (JTOT + 1))

    if first_step:

        @pl.when(chunk == 0)
        def _():
            def put(n, w):
                w_ref[n, 0], w_ref[n, 1] = split(w)

            for k in range(HEL):
                put(k, angular[k].T)
            for k in range(HEL - 1):
                helicity = (lowest + k).astype(F32)
                ladder = coriolis_scale * jnp.sqrt(jnp.full((NA, NA), total_j - helicity * (helicity + 1.0), F32))
                scaled = ladder * coriolis[k]
                put(ABOVE[k], scaled.T)
                put(BELOW[k], scaled)

    parts = [split(now[k].reshape(ROWS, NA)) for k in range(HEL)]

    def product(k, n):
        high, low = parts[k]
        return dot(high, w_ref[n, 0]) + dot(low, w_ref[n, 0]) + dot(high, w_ref[n, 1])

    for k in range(HEL):
        rot[k] = product(k, k)
    mix[0] = product(1, ABOVE[0])
    for k in (1, 2):
        mix[k] = product(k + 1, ABOVE[k]) + product(k - 1, BELOW[k - 1])
    mix[3] = product(2, BELOW[2])

    bond = lax.broadcasted_iota(jnp.int32, (CS, NA), 0)
    diagonal = lax.broadcasted_iota(jnp.int32, (CS, CS), 0) == lax.broadcasted_iota(jnp.int32, (CS, CS), 1)
    live = jnp.where(lax.axis_index("sec") == 0, 1.0, 0.0)

    def factor(position, cells):
        base = 1.0 + 3.0 * position.astype(F32) / float(cells)
        return 1.0 / (base * base)

    bond_cells = lax.axis_size("sr") * CS
    bond_factor = factor(lax.axis_index("sr") * CS + bond, bond_cells)
    radial_cells = lax.axis_size("rr") * CR
    radial_start = lax.axis_index("rr") * CR + first
    helicities = [(lowest + k).astype(F32) for k in range(HEL)]
    centre = [centrifugal * (total_j - 2.0 * h * h) for h in helicities]

    def column(ref, i):
        line = jnp.broadcast_to(ref[pl.ds(i, 1), :], (CS, CS))
        return jnp.sum(jnp.where(diagonal, line, 0.0), axis=1, keepdims=True)

    def row(t):
        i = first + t
        u = factor(jnp.full((CS, NA), radial_start + t, jnp.int32), radial_cells)
        start = t * CS
        damp = jnp.broadcast_to(column(damping, i), (CS, NA))
        share = jnp.broadcast_to(column(switch, i) * live, (CS, NA))
        spin = rotor_scale * (u + bond_factor)
        well = pot[t] + 4.0 * kinetic
        for k in range(HEL):
            v = now[k, t]
            before = now[k, t - 1] if t > 0 else jnp.where(chunk == 0, up[k], above[k, 0])
            after = now[k, t + 1] if t < TI - 1 else jnp.where(chunk == CR // TI - 1, down[k], below[k, 0])
            lower = jnp.where(bond == 0, left[k, pl.ds(i, 1), :], pltpu.roll(v, 1, 0))
            upper = jnp.where(bond == CS - 1, right[k, pl.ds(i, 1), :], pltpu.roll(v, CS - 1, 0))
            applied = (
                (well + u * centre[k]) * v
                - kinetic * ((before + after) + (lower + upper))
                + spin * rot[k, start : start + CS]
                + u * mix[k, start : start + CS]
            )
            renewed = damp * (2.0 * applied - damp * prev[k, t])
            taken = share * renewed
            if want_own:
                own_ref[k, t] = renewed - taken
            if want_pack:
                absorbed[k, i] = taken

    for t in range(TI):
        row(t)

    if first_step:
        for k in range(HEL):
            left_ref[k, pl.ds(pl.multiple_of(first, TI), TI), :] = own_ref[k, :, 0, :]
            right_ref[k, pl.ds(pl.multiple_of(first, TI), TI), :] = own_ref[k, :, CS - 1, :]

        @pl.when(chunk == 0)
        def _():
            top_ref[...] = own_ref[:, 0]

        @pl.when(chunk == CR // TI - 1)
        def _():
            bottom_ref[...] = own_ref[:, TI - 1]

    if want_pack:

        @pl.when(chunk == CR // TI - 1)
        def _():
            def copy(slot, target, to):
                e = jnp.maximum(ids[slot], 0)
                i = e // (CS // BLK)
                j = pl.multiple_of((e % (CS // BLK)) * BLK, BLK)
                for k in range(HEL):
                    target[to, k] = absorbed[k, i, pl.ds(j, BLK), :]

            def move(q, carry):
                half = SRCS // 2
                copy(q + half, pack_zero, q)
                copy(q, pack_zero, q + half)
                for n in range(2):
                    copy(SRCS + half * (n if first_step else 1 - n) + q, pack_one, half * n + q)
                return carry

            lax.fori_loop(0, SRCS // 2, move, 0)


def step_call(first_step, want_own, want_pack, ids, helicity_start, now, halo, prev, pot, damping, switch, *weights, others=()):
    field = (HEL, CR, CS, NA)
    edge = (HEL, CR, NA)
    stack = (10, 2, NA, NA)
    rows = pl.BlockSpec((HEL, TI, CS, NA), lambda c: (0, c, 0, 0))
    out_specs, out_shape, scratch = [], [], []
    if want_own:
        out_specs.append(rows)
        out_shape.append(jax.ShapeDtypeStruct(field, F32))
    if want_pack:
        packed = (SRCS, HEL, BLK, NA)
        out_specs += [whole(packed)] * 2
        out_shape += [jax.ShapeDtypeStruct(packed, F32)] * 2
    if first_step:
        out_specs += [whole(edge)] * 4 + [whole(stack)]
        out_shape += [jax.ShapeDtypeStruct(edge, F32)] * 4 + [jax.ShapeDtypeStruct(stack, BF16)]
    specs, shapes = untouched(others)
    out_specs += specs
    out_shape += shapes
    scratch += [pltpu.VMEM((HEL, ROWS, NA), F32)] * 2
    if want_pack:
        scratch.append(pltpu.VMEM(field, F32))
    weight_specs = [whole((HEL, NA, NA)), whole((HEL - 1, NA, NA))] if first_step else [whole(stack)]
    return pl.pallas_call(
        functools.partial(step_kernel, first_step, want_own, want_pack),
        grid=(CR // TI,),
        in_specs=([smem()] if want_pack else [])
        + [
            smem(),
            rows,
            pl.BlockSpec((HEL, 1, CS, NA), lambda c: (0, jnp.maximum(c * TI - 1, 0), 0, 0)),
            pl.BlockSpec((HEL, 1, CS, NA), lambda c: (0, jnp.minimum(c * TI + TI, CR - 1), 0, 0)),
            whole(edge),
            whole(edge),
            whole(edge),
            whole(edge),
            rows,
            pl.BlockSpec((TI, CS, NA), lambda c: (c, 0, 0)),
            whole((CR, CS)),
            whole((CR, CS)),
        ]
        + weight_specs,
        out_specs=out_specs,
        out_shape=out_shape,
        scratch_shapes=scratch,
        compiler_params=pltpu.CompilerParams(vmem_limit_bytes=56 * MIB),
        cost_estimate=pl.CostEstimate(flops=1000, transcendentals=0, bytes_accessed=1000),
        name="step_first" if first_step else "step_own" if want_own else "step_pack",
    )(*((ids,) if want_pack else ()), helicity_start, now, now, now, *halo, prev, pot, damping, switch, *weights)


def inflow_kernel(count, want_edges, *refs):
    x_refs, refs = refs[:count], refs[count:]
    f_high, f_low, b_high, b_low, acc_ref, *refs = refs
    step = x_refs[0].shape[0] * BLK
    rows_in = count * step
    out_ref = refs[0]
    terms, turned = refs[-2:]
    product_section = lax.axis_index("sec") == 1

    @pl.when(jnp.logical_and(product_section, pl.program_id(0) == 0))
    def _():
        for k in range(HEL):
            lanes = slice(k * NA, (k + 1) * NA)
            for n, x_ref in enumerate(x_refs):
                high, low = split(x_ref[:, k].reshape(step, NA))
                terms[n * step : (n + 1) * step, lanes] = high
                terms[rows_in + n * step : rows_in + (n + 1) * step, lanes] = low

    @pl.when(product_section)
    def _():
        for r in range(rows_in // 256):
            top = slice(r * 256, (r + 1) * 256)
            bottom = slice(rows_in + r * 256, rows_in + (r + 1) * 256)
            framed = dot(terms[top], f_high[0]) + dot(terms[bottom], f_high[0]) + dot(terms[top], f_low[0])
            turned[top], turned[bottom] = split(framed)
        high, low = turned[0:rows_in], turned[rows_in : 2 * rows_in]
        for r in range(PTS // 256):
            rows = slice(r * 256, (r + 1) * 256)
            gain = dot(b_high[rows], high) + dot(b_low[rows], high) + dot(b_high[rows], low)
            lines = slice(r * 256 // CS, (r + 1) * 256 // CS)
            out_ref[0, lines] = acc_ref[0, lines] + gain.reshape(256 // CS, CS, NA)

    @pl.when(jnp.logical_not(product_section))
    def _():
        out_ref[...] = acc_ref[...]

    if want_edges:
        top_ref, bottom_ref, left_ref, right_ref = refs[1:5]
        top_ref[0] = out_ref[0, 0]
        bottom_ref[0] = out_ref[0, CR - 1]
        left_ref[0] = out_ref[0, :, 0, :]
        right_ref[0] = out_ref[0, :, CS - 1, :]


def inflow_call(part, want_edges, xs, frame, blend, acc, flops=1000):
    rows_in = len(xs) * xs[0].shape[0] * BLK
    column = pl.BlockSpec((1, HEL * NA, NA), lambda n: (n, 0, 0))
    weights = pl.BlockSpec((PTS, rows_in), lambda n: (0, part))
    field = pl.BlockSpec((1, CR, CS, NA), lambda n: (n, 0, 0, 0))
    edge = pl.BlockSpec((1, CR, NA), lambda n: (n, 0, 0))
    count = 4 if want_edges else 0
    return pl.pallas_call(
        functools.partial(inflow_kernel, len(xs), want_edges),
        grid=(HEL,),
        in_specs=[whole(x.shape) for x in xs] + [column, column, weights, weights, field],
        out_specs=[field] + [edge] * count,
        out_shape=[jax.ShapeDtypeStruct((HEL, CR, CS, NA), F32)] + [jax.ShapeDtypeStruct((HEL, CR, NA), F32)] * count,
        scratch_shapes=[pltpu.VMEM((2 * rows_in, HEL * NA), BF16), pltpu.VMEM((2 * rows_in, NA), BF16)],
        compiler_params=pltpu.CompilerParams(vmem_limit_bytes=56 * MIB),
        cost_estimate=pl.CostEstimate(flops=flops, transcendentals=0, bytes_accessed=1000),
        name="inflow_edges" if want_edges else "inflow",
    )(*xs, *frame, *blend, acc)


def exchange(top, bottom, left, right):
    rows, columns = lax.axis_size("rr"), lax.axis_size("sr")

    def send(piece, axis, peers, forward):
        pairs = [(i, i + 1) if forward else (i + 1, i) for i in range(peers - 1)]
        return lax.ppermute(piece, axis, pairs)

    return (
        send(bottom, "rr", rows, True),
        send(top, "rr", rows, False),
        send(right, "sr", columns, True),
        send(left, "sr", columns, False),
    )


def cross(x):
    pairs = [(s, SRCS + (s ^ (SRCS // 2))) for s in range(SRCS)]
    return lax.ppermute(x, ALL, pairs)


def spread(x):
    return lax.all_to_all(x, ("rr", "sr"), split_axis=0, concat_axis=0, tiled=True)


def per_device(
    wave_prev,
    wave_now,
    potential,
    damping,
    switch,
    angular,
    coriolis,
    helicity_start,
    frame_map,
    route_table,
    pick_slots,
    interp_weights,
):
    section = lax.axis_index("sec")
    me = lax.axis_index("rr") * lax.axis_size("sr") + lax.axis_index("sr")
    previous, current = wave_prev[0], wave_now[0]
    halo = exchange(current[:, 0], current[:, CR - 1], current[:, :, 0], current[:, :, CS - 1])
    outgoing = lax.dynamic_index_in_dim(route_table, me, axis=1, keepdims=False)
    ids = outgoing.T.reshape(2 * SRCS)

    fixed = (potential[0], damping[0], switch)

    own_1, one_1, zero_1, *rims, weights = step_call(
        True, True, True, ids, helicity_start, current, halo, previous, *fixed, angular[0], coriolis[0]
    )
    crossed_one_1 = cross(one_1)
    halo = exchange(*rims)
    relayed_1 = spread(zero_1)
    pack_shapes = [jax.ShapeDtypeStruct((SRCS, HEL, BLK, NA), F32)] * 2
    blend_shapes = [jax.ShapeDtypeStruct((PTS, PTS), BF16)] * 2

    def reactant(own, halo, weights, *_):
        one, zero, *rest = step_call(
            False, False, True, ids, helicity_start, own, halo, current, *fixed, weights, others=blend_shapes
        )
        return one, zero, tuple(rest)

    def product(own, halo, weights, picks, tiles):
        high, low, one, zero = blend_call(picks, tiles, pack_shapes)
        return one, zero, (high, low)

    late_map, late_weights, own_1 = lax.optimization_barrier((frame_map, interp_weights[0, 0], own_1))
    frame, tiles = frame_terms(late_map), jnp.tile(late_weights, (1, 1, 1, 128 // BLK))
    own_1, frame, tiles, relayed_1 = lax.optimization_barrier((own_1, frame, tiles, relayed_1))
    crossed_zero_1 = cross(relayed_1)
    picks = pick_slots[0, 0].T.reshape(MSLOT * NBLK)
    one_2, zero_2, blend = lax.cond(section == 0, reactant, product, own_1, halo, weights, picks, tiles)
    shared = spread(jnp.where(section == 0, zero_2, crossed_one_1))
    crossed_zero_2 = cross(shared)
    one_2, shared = lax.optimization_barrier((one_2, shared))
    relayed_2 = spread(one_2)

    new_1, *rims = inflow_call(0, True, (crossed_zero_1, shared), frame, blend, own_1, 40 << 30)
    relayed_2, rims = lax.optimization_barrier((relayed_2, rims))
    first_2, last_2 = cross(relayed_2[: SRCS // 2]), cross(relayed_2[SRCS // 2 :])
    halo = exchange(*rims)
    (own_2,) = step_call(False, True, False, ids, helicity_start, new_1, halo, current, *fixed, weights)
    (new_2,) = inflow_call(0, False, (crossed_zero_2,), frame, blend, own_2)
    (new_2,) = inflow_call(3, False, (first_2,), frame, blend, new_2)
    (new_2,) = inflow_call(2, False, (last_2,), frame, blend, new_2)
    return new_1[None], new_2[None]


def solution(mesh):
    placed = (
        P("sec", None, "rr", "sr", None),
        P("sec", None, "rr", "sr", None),
        P("sec", "rr", "sr", None),
        P("sec", "rr", "sr"),
        P("rr", "sr"),
        P("sec", None, None, None),
        P("sec", None, None, None),
        P("sec"),
        P(),
        P(),
        P("rr", "sr", None, None),
        P("rr", "sr", None, None, None, None),
    )
    return jax.shard_map(
        per_device,
        mesh=mesh,
        in_specs=placed,
        out_specs=(P("sec", None, "rr", "sr", None), P("sec", None, "rr", "sr", None)),
        check_vma=False,
    )
```
